256 devices in a mesh: gx: 16 (over x, y), gy: 16 (over z, core).
Axes of the slice: x: 4, y: 4, z: 8, core: 2. Of those that a mesh axis runs over, the one named last changes fastest.
Arguments:
- velocity: bfloat16 [3, 256, 512, 256], P(None, 'gx', 'gy'), may hold values from -4 to 4
- density: bfloat16 [256, 512, 256], P('gx', 'gy'), may hold values from 0 to 1
Outputs:
- projected: float32 [3, 256, 512, 256], P(None, 'gx', 'gy')
- emission: float32 [256, 512, 256], P('gx', 'gy')
The draws below stay inside these ranges and needn't reach their ends.
All inputs are finite; a program needn't handle non-finite values.
Results may differ from the reference program's by a relative error of at most 0.0003.
Values sent between devices are 32-bit elements; how exact they have to be, the bound alone decides.
No kernel may reach another device: no remote copies, remote signals or barrier semaphores. Data moves between devices by JAX's collectives and lax.ppermute only.
A program may use at most 64 MiB of HBM per device.

```python
import jax
import jax.numpy as jnp
from jax import lax

NZ = 256
NX = 256
NY = 512


def levels(rng, dims, pieces, low, top_value):
    def one(axis_at, blocks):
        steps = jax.random.uniform(jax.random.fold_in(jax.random.fold_in(rng, 6), axis_at), (blocks,), jnp.float32, low / len(pieces), top_value / len(pieces))
        return jnp.repeat(jnp.exp(steps), dims[axis_at] // blocks).reshape((-1,) + (1,) * (len(dims) - axis_at - 1))

    factor_of = one(*pieces[0])
    for cut in pieces[1:]:
        factor_of = factor_of * one(*cut)
    return factor_of


def scatter_about(stream_key, dims, deviation, reach, split=(), kind=jnp.bfloat16):
    entries = jax.random.normal(stream_key, dims, jnp.float32) * deviation
    if len(split) > 0:
        entries = levels(stream_key, dims, split, -0.22, 0.18) * entries
    return jnp.clip(entries, min=-reach, max=reach).astype(kind)


def setup_inputs(seed: int = 0) -> dict:
    splits = jax.random.split(jax.random.key(seed), 3)
    velocity = scatter_about(splits[0], (3, NX, NY, NZ), 1.0, 4.0, ((1, 16), (2, 16)))
    density = jnp.clip(1.0 * jax.random.uniform(splits[1], (NX, NY, NZ), jnp.float32) ** levels(splits[1], (NX, NY, NZ), ((0, 16), (1, 16)), -0.2, 0.2), 0.0, 1.0).astype(jnp.bfloat16)
    return {"velocity": velocity, "density": density}


time_step = 0.4
buoyancy = 2.0
extinction = 3.0
highest = lax.Precision.HIGHEST

def cosine_table(length):
    modes = jnp.arange(length, dtype=jnp.float32)[:, None]
    centres = jnp.arange(length, dtype=jnp.float32)[None, :] + 0.5
    factor = jnp.where(modes == 0, jnp.sqrt(1.0 / length), jnp.sqrt(2.0 / length))
    return (factor * jnp.cos(jnp.pi * modes * centres / length)).astype(jnp.float32)

def flux_terms(padded):
    extent = padded.shape

    def window(offset_x, offset_y, offset_z):
        return padded[:, 2 + offset_x:extent[1] - 2 + offset_x, 2 + offset_y:extent[2] - 2 + offset_y, 2 + offset_z:extent[3] - 2 + offset_z]

    def moved(axis_id, offset):
        offsets = [0, 0, 0]
        offsets[axis_id] = offset
        return window(offsets[0], offsets[1], offsets[2])
    middle = window(0, 0, 0)
    summed = jnp.zeros_like(middle)
    for axis_id in range(3):
        plus_one = moved(axis_id, 1)
        plus_two = moved(axis_id, 2)
        minus_one = moved(axis_id, -1)
        minus_two = moved(axis_id, -2)
        lower_diff = (2.0 * plus_one + 3.0 * middle - 6.0 * minus_one + minus_two) / 6.0
        upper_diff = (-plus_two + 6.0 * plus_one - 3.0 * middle - 2.0 * minus_one) / 6.0
        speed_axis = middle[axis_id]
        summed = summed + jnp.maximum(speed_axis, 0.0) * lower_diff + jnp.minimum(speed_axis, 0.0) * upper_diff
    return -summed

def close_walls(fields):
    open_x = (jnp.arange(NX) < NX - 1)[:, None, None]
    open_y = (jnp.arange(NY) < NY - 1)[None, :, None]
    open_z = (jnp.arange(NZ) < NZ - 1)[None, None, :]
    return jnp.stack([fields[0] * open_x, fields[1] * open_y, fields[2] * open_z, fields[3]])

def eigen_row(length):
    modes = jnp.arange(length, dtype=jnp.float32)
    return 2.0 - 2.0 * jnp.cos(jnp.pi * modes / length)

def reference(velocity, density):
    fields = jnp.concatenate([velocity.astype(jnp.float32), density.astype(jnp.float32)[None]], axis=0)
    margins = ((0, 0), (2, 2), (2, 2), (2, 2))
    section_one = close_walls(fields + time_step * flux_terms(jnp.pad(fields, margins)))
    section_two = close_walls(0.5 * fields + 0.5 * (section_one + time_step * flux_terms(jnp.pad(section_one, margins))))
    smoke_now = section_two[3]
    smoke_above = jnp.concatenate([smoke_now[:, :, 1:], jnp.zeros_like(smoke_now[:, :, :1])], axis=2)
    lifted = close_walls(jnp.stack([section_two[0], section_two[1], section_two[2] + time_step * buoyancy * 0.5 * (smoke_now + smoke_above), smoke_now]))
    below_x = jnp.concatenate([jnp.zeros_like(lifted[0][:1]), lifted[0][:-1]], axis=0)
    below_y = jnp.concatenate([jnp.zeros_like(lifted[1][:, :1]), lifted[1][:, :-1]], axis=1)
    below_z = jnp.concatenate([jnp.zeros_like(lifted[2][:, :, :1]), lifted[2][:, :, :-1]], axis=2)
    divergence = lifted[0] - below_x + (lifted[1] - below_y) + (lifted[2] - below_z)
    table_x = cosine_table(NX)
    table_y = cosine_table(NY)
    table_z = cosine_table(NZ)
    spectrum = jnp.einsum('xyn,kn->xyk', divergence, table_z, precision=highest)
    spectrum = jnp.einsum('xyk,ix->iyk', spectrum, table_x, precision=highest)
    spectrum = jnp.einsum('iyk,jy->ijk', spectrum, table_y, precision=highest)
    eigen_sum = eigen_row(NZ)[None, None, :] + eigen_row(NX)[:, None, None] + eigen_row(NY)[None, :, None]
    zero_mode = ((jnp.arange(NX) == 0)[:, None, None] & (jnp.arange(NY) == 0)[None, :, None] & (jnp.arange(NZ) == 0)[None, None, :]).astype(jnp.float32)
    pressure_hat = -spectrum * (1.0 - zero_mode) / (eigen_sum + zero_mode)
    pressure = jnp.einsum('ijk,ix->xjk', pressure_hat, table_x, precision=highest)
    pressure = jnp.einsum('xjk,jy->xyk', pressure, table_y, precision=highest)
    pressure = jnp.einsum('xyk,kn->xyn', pressure, table_z, precision=highest)
    grad_x = jnp.concatenate([pressure[1:], jnp.zeros_like(pressure[:1])], axis=0) - pressure
    grad_y = jnp.concatenate([pressure[:, 1:], jnp.zeros_like(pressure[:, :1])], axis=1) - pressure
    grad_z = jnp.concatenate([pressure[:, :, 1:], jnp.zeros_like(pressure[:, :, :1])], axis=2) - pressure
    projected = close_walls(jnp.stack([lifted[0] - grad_x, lifted[1] - grad_y, lifted[2] - grad_z, lifted[3]]))[:3]
    attenuation = extinction / NX
    optical = attenuation * (jnp.cumsum(smoke_now, axis=0) - smoke_now)
    emission = jnp.exp(-optical) * -jnp.expm1(-attenuation * smoke_now) / attenuation
    return (projected, emission)
```

```python
import functools

import jax
import jax.numpy as jnp
import numpy as np
from jax import lax
from jax.experimental import pallas as pl
from jax.experimental.pallas import tpu as pltpu
from jax.sharding import PartitionSpec as P

time_step = 0.4
buoyancy = 2.0
extinction = 3.0
highest = lax.Precision.HIGHEST


def padded_2(block, sides, width):
    for axis, dim in sides:
        count = lax.axis_size(axis)
        forward = [(i, i + 1) for i in range(count - 1)]
        backward = [(target, source) for source, target in forward]
        low = lax.ppermute(
            lax.slice_in_dim(block, block.shape[dim] - width, None, axis=dim), axis, forward
        )
        high = lax.ppermute(lax.slice_in_dim(block, 0, width, axis=dim), axis, backward)
        block = jnp.concatenate([low, block, high], axis=dim)
    return block


block_x, block_y, size_z = 16, 32, 256
count_x, count_y = 16, 16
full_x, full_y = 256, 512
chunk_z = 16
send_rows = 72
back_rows = 88


def cosine_array(length):
    modes = np.arange(length, dtype=np.float64)[:, None]
    centres = np.arange(length, dtype=np.float64)[None, :] + 0.5
    factor = np.where(modes == 0, np.sqrt(1.0 / length), np.sqrt(2.0 / length))
    return (factor * np.cos(np.pi * modes * centres / length)).astype(np.float32)


def eigen_array(length):
    modes = np.arange(length, dtype=np.float64)
    return (4.0 * np.sin(np.pi * modes / (2 * length)) ** 2).astype(np.float32)


def swap_groups(tile):
    row = lax.broadcasted_iota(jnp.int32, (8, 128), 0)
    group = lax.broadcasted_iota(jnp.int32, (8, 128), 1) // 16
    for step in (1, 2, 4):
        row_bit = (row & step) != 0
        group_bit = (group & step) != 0
        below = pltpu.roll(pltpu.roll(tile, 8 - step, 0), 16 * step, 1)
        above = pltpu.roll(pltpu.roll(tile, step, 0), 128 - 16 * step, 1)
        tile = jnp.where(
            row_bit == group_bit, tile, jnp.where(group_bit, below, above)
        )
    return tile


def dot(left, right, dims):
    return lax.dot_general(
        left, right, (dims, ((), ())), precision=highest, preferred_element_type=jnp.float32
    )


def pack_kernel(div_ref, smoke_ref, table_ref, out_ref, freq_ref, total_ref):
    freq_ref[...] = dot(
        div_ref[...].reshape(block_x * block_y, size_z), table_ref[...], ((1,), (0,))
    )

    def add_plane(x, total):
        return total + smoke_ref[x]

    total_ref[...] = lax.fori_loop(0, block_x, add_plane, jnp.zeros((block_y, size_z), jnp.float32))

    def one(x, carry):
        for part in range(4):
            for half in range(2):
                tile = freq_ref[
                    pl.ds(pl.multiple_of(x * block_y, 8) + part * 8, 8), half * 128 : half * 128 + 128
                ]
                out_ref[pl.ds(half * 8 * send_rows + part * 16 + x, 8, stride=send_rows), :] = (
                    swap_groups(tile)
                )
        return carry

    lax.fori_loop(0, block_x, one, 0)
    for part in range(4):
        for half in range(2):
            tile = total_ref[part * 8 : part * 8 + 8, half * 128 : half * 128 + 128]
            out_ref[pl.ds(half * 8 * send_rows + 64 + part, 8, stride=send_rows), :] = swap_groups(
                tile
            )
    for peer in range(count_x):
        out_ref[peer * send_rows + 68 : peer * send_rows + 72, :] = jnp.zeros((4, 128), jnp.float32)


def power_of(base, exponent, bits):
    result = jnp.ones_like(base)
    for bit in range(bits):
        result = jnp.where((exponent >> bit) & 1 == 1, result * base, result)
        base = base * base
    return result


def roots_of(lam):
    half = 0.5 * lam
    spread = jnp.sqrt(lam + half * half)
    rho = 1.0 / (1.0 + half + spread)
    return rho, spread


def squared(value, times):
    for _ in range(times):
        value = value * value
    return value


def forward_kernel(place_ref, got_ref, lam_ref, table_ref, local_ref, ends_ref, send_ref, before_ref, line_ref):
    place_y = place_ref[1]
    for part in range(4):
        lines = got_ref[:, part * 16 : part * 16 + 16, :].reshape(full_x, 128)
        line_ref[part * 128 : part * 128 + 128, :] = dot(lines, table_ref[...], ((0,), (0,)))
    lam = lam_ref[...]
    rho, _ = roots_of(lam)
    special = lam == 0.0
    low = jnp.zeros((chunk_z, full_x), jnp.float32)
    for y in range(block_y):
        low = low * rho + line_ref[y * 16 : y * 16 + 16, :]
        local_ref[y * 16 : y * 16 + 16, :] = low
    high = jnp.zeros((chunk_z, full_x), jnp.float32)
    for y in reversed(range(block_y)):
        high = high * rho
        rows = slice(y * 16, y * 16 + 16)
        here = local_ref[rows, :]
        local_ref[rows, :] = jnp.where(special, here, here + high)
        high = high + line_ref[rows, :]
    ends_ref[0] = low
    ends_ref[1] = high
    rho_32 = squared(rho, 5)
    rho_64 = rho_32 * rho_32
    up = low + power_of(rho_64, place_y, 4) * rho_32 * high
    down = high + power_of(rho_64, count_y - 1 - place_y, 4) * rho_32 * low
    for peer in range(count_y):
        send_ref[peer] = jnp.where(peer > place_y, up, down)
    running = jnp.zeros((4, 128), jnp.float32)
    for peer in range(count_x):
        before_ref[peer, 0:4, :] = running
        running = running + got_ref[peer, 64:68, :]


def backward_kernel(
    place_ref, local_ref, ends_ref, got_ref, lam_ref, table_ref, next_ref, before_ref, out_ref, line_ref
):
    place_y = place_ref[1]
    lam = lam_ref[...]
    rho, spread = roots_of(lam)
    special = lam == 0.0
    scale = jnp.where(special, 0.0, -0.5 / jnp.where(special, 1.0, spread))
    low, high = ends_ref[0], ends_ref[1]
    rho_32 = squared(rho, 5)
    rho_64 = rho_32 * rho_32
    rho_up = power_of(rho_64, place_y, 4)
    rho_down = power_of(rho_64, count_y - 1 - place_y, 4)
    from_low = jnp.zeros((chunk_z, full_x), jnp.float32)
    from_high = jnp.zeros((chunk_z, full_x), jnp.float32)
    for peer in range(count_y):
        from_low = jnp.where(peer < place_y, from_low * rho_32 + got_ref[peer], from_low)
        other = count_y - 1 - peer
        from_high = jnp.where(other > place_y, from_high * rho_32 + got_ref[other], from_high)
    rho_992 = rho_up * rho_down * rho_32
    wrap = 1.0 / jnp.where(special, 1.0, 1.0 - rho_992 * rho_32)
    enter_low = (from_low + rho_up * (rho_32 * from_high + high) + rho_992 * low) * wrap
    enter_high = (from_high + rho_down * (rho_32 * from_low + low) + rho_992 * high) * wrap
    mean = (0.5 * (from_low + from_high) + low) * (1.0 / full_y)
    flux_in = 0.5 * from_low - mean * (place_y * block_y).astype(jnp.float32)
    for y in reversed(range(block_y)):
        enter_high_next = enter_high
        rows = slice((y + 1) * 16, (y + 1) * 16 + 16)
        if y + 1 == block_y:
            line_ref[rows, :] = rho * low + enter_high_next
        else:
            line_ref[rows, :] = local_ref[rows, :] + jnp.where(special, 0.0, enter_high_next)
        enter_high = enter_high * rho
    line_ref[0:16, :] = local_ref[0:16, :] + jnp.where(special, 0.0, enter_high)
    level = jnp.zeros((chunk_z, full_x), jnp.float32)
    for y in range(block_y + 1):
        rows = slice(y * 16, y * 16 + 16)
        enter_low = enter_low * rho
        here = line_ref[rows, :]
        line_ref[rows, :] = jnp.where(special, level, scale * (here + enter_low))
        level = level + (here + flux_in - mean * (y + 1.0))
    line_ref[(block_y + 1) * 16 :, :] = jnp.zeros((112, full_x), jnp.float32)
    for part in range(5):
        lines = line_ref[part * 128 : part * 128 + 128, :]
        out_ref[:, part * 16 : part * 16 + 16, :] = dot(table_ref[...], lines, ((1,), (1,))).reshape(
            count_x, block_x, 128
        )
        if part < 4:
            out_ref[:, 80 + part : 81 + part, :] = dot(next_ref[...], lines, ((1,), (1,))).reshape(
                count_x, 1, 128
            )
    out_ref[:, 84:88, :] = before_ref[:, 0:4, :]


def final_kernel(place_ref, got_ref, lifted_ref, smoke_ref, table_ref, out_ref, glow_ref, freq_ref, press_ref):
    place_x, place_y = place_ref[0], place_ref[1]

    def tile_at(row, half):
        return swap_groups(got_ref[pl.ds(half * 8 * back_rows + row, 8, stride=back_rows), :])

    def one(x, carry):
        for part in range(5):
            for half in range(2):
                freq_ref[x, part * 8 : part * 8 + 8, half * 128 : half * 128 + 128] = tile_at(
                    part * 16 + x, half
                )
        return carry

    lax.fori_loop(0, block_x, one, 0)
    for part in range(4):
        for half in range(2):
            freq_ref[block_x, part * 8 : part * 8 + 8, half * 128 : half * 128 + 128] = tile_at(
                80 + part, half
            )
    freq_ref[block_x, 32:40, :] = jnp.zeros((8, size_z), jnp.float32)
    press_ref[...] = dot(
        freq_ref[...].reshape((block_x + 1) * 40, size_z), table_ref[...], ((1,), (0,))
    ).reshape(block_x + 1, 40, size_z)
    along_y = lax.broadcasted_iota(jnp.int32, (block_y, size_z), 0) + place_y * block_y
    along_z = lax.broadcasted_iota(jnp.int32, (block_y, size_z), 1)
    open_y = along_y < full_y - 1
    open_z = along_z < size_z - 1
    entered = jnp.concatenate(
        [
            jnp.concatenate([tile_at(84 + part, half) for half in range(2)], axis=1)
            for part in range(4)
        ],
        axis=0,
    )
    attenuation = extinction / full_x

    def finish(x, running):
        here = press_ref[x, 0:block_y, :]
        open_x = place_x * block_x + x < full_x - 1
        out_ref[0, x] = jnp.where(
            open_x, lifted_ref[0, x] - (press_ref[x + 1, 0:block_y, :] - here), 0.0
        )
        out_ref[1, x] = jnp.where(
            open_y, lifted_ref[1, x] - (press_ref[x, 1 : block_y + 1, :] - here), 0.0
        )
        out_ref[2, x] = jnp.where(
            open_z, lifted_ref[2, x] - (pltpu.roll(here, size_z - 1, 1) - here), 0.0
        )
        smoke = smoke_ref[x]
        depth = attenuation * smoke
        series = 1.0 - depth * (1.0 / 7.0)
        for order in (6.0, 5.0, 4.0, 3.0, 2.0):
            series = 1.0 - depth * (1.0 / order) * series
        lost = jnp.where(jnp.abs(depth) < 0.25, depth * series, 1.0 - jnp.exp(-depth))
        glow_ref[x] = jnp.exp(-attenuation * running) * lost * (1.0 / attenuation)
        return running + smoke

    lax.fori_loop(0, block_x, finish, entered)


def shaped(*dims):
    return jax.ShapeDtypeStruct(dims, jnp.float32)


def call(kernel, outs, scratch, scalars=True):
    vmem = pl.BlockSpec(memory_space=pltpu.VMEM)

    def run(*args):
        specs = [vmem] * len(args)
        if scalars:
            specs[0] = pl.BlockSpec(memory_space=pltpu.SMEM)
        return pl.pallas_call(
            kernel,
            out_shape=outs,
            in_specs=specs,
            out_specs=jax.tree.map(lambda _: vmem, outs),
            scratch_shapes=[pltpu.VMEM(dims, jnp.float32) for dims in scratch],
            name=kernel.__name__,
        )(*args)

    return run


def project(place_x, place_y, lifted, divergence, smoke):
    place = jnp.stack([place_x, place_y]).astype(jnp.int32)
    table_z = cosine_array(size_z)
    table_x = cosine_array(full_x)
    next_x = np.concatenate(
        [table_x.T[block_x::block_x], np.zeros((1, full_x), np.float32)], axis=0
    )
    lam = (
        lax.dynamic_slice_in_dim(jnp.asarray(eigen_array(size_z)), place_x * chunk_z, chunk_z)[:, None]
        + jnp.asarray(eigen_array(full_x))[None, :]
    )
    packed = call(
        pack_kernel,
        shaped(count_x * send_rows, 128),
        [(block_x * block_y, size_z), (block_y, size_z)],
        scalars=False,
    )(divergence, smoke, jnp.asarray(np.ascontiguousarray(table_z.T)))
    got = lax.all_to_all(
        packed.reshape(count_x, send_rows, 128), "gx", split_axis=0, concat_axis=0, tiled=True
    )
    table_xt = jnp.asarray(np.ascontiguousarray(table_x.T))
    local, ends, moments, before = call(
        forward_kernel,
        (
            shaped(block_y * chunk_z, full_x),
            shaped(2, chunk_z, full_x),
            shaped(count_y, chunk_z, full_x),
            shaped(count_x, 8, 128),
        ),
        [(block_y * chunk_z, full_x)],
    )(place, got, lam, table_xt)
    moments = lax.all_to_all(moments, "gy", split_axis=0, concat_axis=0, tiled=True)
    back = call(
        backward_kernel,
        shaped(count_x, back_rows, 128),
        [(5 * 128, full_x)],
    )(place, local, ends, moments, lam, table_xt, jnp.asarray(next_x), before)
    back = lax.all_to_all(back, "gx", split_axis=0, concat_axis=0, tiled=True)
    return call(
        final_kernel,
        (shaped(3, block_x, block_y, size_z), shaped(block_x, block_y, size_z)),
        [(block_x + 1, 40, size_z), (block_x + 1, 40, size_z)],
    )(place, back.reshape(count_x * back_rows, 128), lifted, smoke, jnp.asarray(table_z))


def flux_terms(padded):
    extent = padded.shape

    def window(offset_x, offset_y, offset_z):
        return padded[
            :,
            2 + offset_x : extent[1] - 2 + offset_x,
            2 + offset_y : extent[2] - 2 + offset_y,
            2 + offset_z : extent[3] - 2 + offset_z,
        ]

    def moved(axis_id, offset):
        offsets = [0, 0, 0]
        offsets[axis_id] = offset
        return window(offsets[0], offsets[1], offsets[2])

    middle = window(0, 0, 0)
    summed = jnp.zeros_like(middle)
    for axis_id in range(3):
        plus_one = moved(axis_id, 1)
        plus_two = moved(axis_id, 2)
        minus_one = moved(axis_id, -1)
        minus_two = moved(axis_id, -2)
        lower_diff = (2.0 * plus_one + 3.0 * middle - 6.0 * minus_one + minus_two) / 6.0
        upper_diff = (-plus_two + 6.0 * plus_one - 3.0 * middle - 2.0 * minus_one) / 6.0
        speed_axis = middle[axis_id]
        summed = (
            summed
            + jnp.maximum(speed_axis, 0.0) * lower_diff
            + jnp.minimum(speed_axis, 0.0) * upper_diff
        )
    return -summed


def tendency_rim(extended):
    return flux_terms(jnp.pad(extended, ((0, 0), (0, 0), (0, 0), (2, 2))))


def cropped(extended, have_rim, want_rim):
    cut_size = have_rim - want_rim
    return extended[
        :, cut_size : extended.shape[1] - cut_size, cut_size : extended.shape[2] - cut_size, :
    ]


def advect_halo(fields, rim_width):
    return padded_2(fields, (("gx", 1), ("gy", 2)), rim_width)


def per_device(velocity, density):
    block_x, block_y, length_z = density.shape
    count_x = lax.axis_size("gx")
    count_y = lax.axis_size("gy")
    full_x = block_x * count_x
    full_y = block_y * count_y
    anchor_x = lax.axis_index("gx") * block_x
    anchor_y = lax.axis_index("gy") * block_y


    def confine(fields, rim_width):
        along_x = anchor_x - rim_width + jnp.arange(block_x + 2 * rim_width)
        along_y = anchor_y - rim_width + jnp.arange(block_y + 2 * rim_width)
        along_z = jnp.arange(length_z)
        inside = ((along_x >= 0) & (along_x < full_x))[:, None, None] & (
            (along_y >= 0) & (along_y < full_y)
        )[None, :, None]
        open_x = inside & (along_x < full_x - 1)[:, None, None]
        open_y = inside & (along_y < full_y - 1)[None, :, None]
        open_z = inside & (along_z < length_z - 1)[None, None, :]
        return jnp.stack(
            [fields[0] * open_x, fields[1] * open_y, fields[2] * open_z, fields[3] * inside]
        )

    fields = jnp.concatenate(
        [velocity.astype(jnp.float32), density.astype(jnp.float32)[None]], axis=0
    )
    widened = advect_halo(fields, 2)
    section_one = confine(fields + time_step * tendency_rim(widened), 0)
    section_one = advect_halo(section_one, 3)
    earlier = cropped(widened, 2, 1)
    section_two = confine(
        0.5 * earlier + 0.5 * (cropped(section_one, 3, 1) + time_step * tendency_rim(section_one)),
        1,
    )
    smoke_now = section_two[3]
    smoke_above = jnp.concatenate(
        [smoke_now[:, :, 1:], jnp.zeros_like(smoke_now[:, :, :1])], axis=2
    )
    lifted = confine(
        jnp.stack(
            [
                section_two[0],
                section_two[1],
                section_two[2] + time_step * buoyancy * 0.5 * (smoke_now + smoke_above),
                smoke_now,
            ]
        ),
        1,
    )
    interior = lifted[:, 1:-1, 1:-1, :]
    below_z = jnp.concatenate(
        [jnp.zeros_like(interior[2][:, :, :1]), interior[2][:, :, :-1]], axis=2
    )
    divergence = (
        interior[0]
        - lifted[0, :-2, 1:-1, :]
        + (interior[1] - lifted[1, 1:-1, :-2, :])
        + (interior[2] - below_z)
    )
    return project(
        lax.axis_index("gx"), lax.axis_index("gy"), interior, divergence, interior[3]
    )


def solution(mesh):
    in_specs = (P(None, "gx", "gy", None), P("gx", "gy", None))
    out_specs = (P(None, "gx", "gy", None), P("gx", "gy", None))
    return jax.shard_map(
        per_device, mesh=mesh, in_specs=in_specs, out_specs=out_specs, check_vma=False
    )
```

```python
import jax
import jax.numpy as jnp
import numpy as np
from jax import lax
from jax.experimental import pallas as pl
from jax.experimental.pallas import tpu as pltpu
from jax.sharding import PartitionSpec as P

time_step = 0.4
buoyancy = 2.0
extinction = 3.0
highest = lax.Precision.HIGHEST

block_x, block_y, size_z = 16, 32, 256
count_x, count_y = 16, 16
full_x, full_y = 256, 512
chunk_z = 16
send_rows = 72
back_rows = 88


def cosine_array(length):
    modes = np.arange(length, dtype=np.float64)[:, None]
    centres = np.arange(length, dtype=np.float64)[None, :] + 0.5
    factor = np.where(modes == 0, np.sqrt(1.0 / length), np.sqrt(2.0 / length))
    return (factor * np.cos(np.pi * modes * centres / length)).astype(np.float32)


def eigen_array(length):
    modes = np.arange(length, dtype=np.float64)
    return (4.0 * np.sin(np.pi * modes / (2 * length)) ** 2).astype(np.float32)


def swap_groups(tile):
    row = lax.broadcasted_iota(jnp.int32, (8, 128), 0)
    group = lax.broadcasted_iota(jnp.int32, (8, 128), 1) // 16
    for step in (1, 2, 4):
        row_bit = (row & step) != 0
        group_bit = (group & step) != 0
        below = pltpu.roll(pltpu.roll(tile, 8 - step, 0), 16 * step, 1)
        above = pltpu.roll(pltpu.roll(tile, step, 0), 128 - 16 * step, 1)
        tile = jnp.where(
            row_bit == group_bit, tile, jnp.where(group_bit, below, above)
        )
    return tile


def dot(left, right, dims):
    return lax.dot_general(
        left, right, (dims, ((), ())), precision=highest, preferred_element_type=jnp.float32
    )


def weights(speeds, step, z_masks):
    taps = []
    centre = None
    for axis, speed in enumerate(speeds):
        scaled = speed * (step / 6.0)
        ahead = jnp.maximum(scaled, 0.0)
        back = ahead - scaled
        centre = ahead + back if centre is None else centre + (ahead + back)
        plus_one = 6.0 * back - 2.0 * ahead
        minus_one = 6.0 * ahead - 2.0 * back
        if axis == 2:
            plus_two, plus_one, minus_one, minus_two = (
                jnp.where(mask, part, 0.0)
                for mask, part in zip(z_masks, (back, plus_one, minus_one, ahead))
            )
            taps.append((plus_two, plus_one, minus_one, minus_two))
        else:
            taps.append((back, plus_one, minus_one, ahead))
    return taps, -3.0 * centre


def moved_by(ref, field, x, row, taps, centre, middle):
    total = centre * middle
    for axis, (plus_two, plus_one, minus_one, minus_two) in enumerate(taps):
        if axis == 0:
            parts = [ref[field, x + shift, row : row + 8, :] for shift in (2, 1, -1, -2)]
        elif axis == 1:
            parts = [ref[field, x, row + shift : row + shift + 8, :] for shift in (2, 1, -1, -2)]
        else:
            parts = [pltpu.roll(middle, (256 - shift) % 256, 1) for shift in (2, 1, -1, -2)]
        total = total - plus_two * parts[0]
        total = total + plus_one * parts[1]
        total = total + minus_one * parts[2]
        total = total - minus_two * parts[3]
    return total


def advect_kernel(
    place_ref, velocity_ref, density_ref, low_x_ref, high_x_ref, low_y_ref, high_y_ref, low_c_ref,
    high_c_ref, table_ref, lifted_ref, smoke_ref, out_ref,
    raw_ref, one_ref, line_ref, below_ref, div_ref, freq_ref, total_ref,
):
    place_x, place_y = place_ref[0], place_ref[1]

    def fill(x, carry):
        for field in range(4):
            source = velocity_ref[field, x] if field < 3 else density_ref[x]
            raw_ref[field, x + 5, 16:48, :] = source.astype(jnp.float32)
            raw_ref[field, x + 5, 8:16, :] = low_y_ref[field, x]
            raw_ref[field, x + 5, 48:56, :] = high_y_ref[field, x]
        return carry

    lax.fori_loop(0, block_x, fill, 0)
    for field in range(4):
        for x in range(4):
            raw_ref[field, x + 1, 16:48, :] = low_x_ref[field * 4 + x]
            raw_ref[field, x + 1, 12:16, :] = low_c_ref[field, x, 0:4, :]
            raw_ref[field, x + 1, 48:52, :] = low_c_ref[field, x, 4:8, :]
            raw_ref[field, x + 21, 16:48, :] = high_x_ref[field * 4 + x]
            raw_ref[field, x + 21, 12:16, :] = high_c_ref[field, x, 0:4, :]
            raw_ref[field, x + 21, 48:52, :] = high_c_ref[field, x, 4:8, :]
    raw_ref[0, 0, 16:48, :] = low_x_ref[16]

    lane = lax.broadcasted_iota(jnp.int32, (8, size_z), 1)
    row_of = lax.broadcasted_iota(jnp.int32, (8, size_z), 0)
    z_masks = (lane < size_z - 2, lane < size_z - 1, lane > 0, lane > 1)
    open_z = z_masks[1]

    def closed(value, field, open_x, row):
        if field == 0:
            return jnp.where(open_x, value, 0.0)
        if field == 1:
            return jnp.where(place_y * block_y + (row - 16) + row_of != full_y - 1, value, 0.0)
        if field == 2:
            return jnp.where(open_z, value, 0.0)
        return value

    def section_one(x, carry):
        open_x = place_x * block_x + x - 3 != full_x - 1
        for row in range(8, 56, 8):
            middles = [raw_ref[field, x + 2, row : row + 8, :] for field in range(4)]
            taps, centre = weights(middles[:3], time_step, z_masks)
            for field in range(4):
                value = middles[field] + moved_by(
                    raw_ref, field, x + 2, row, taps, centre, middles[field]
                )
                one_ref[field, x, row : row + 8, :] = closed(value, field, open_x, row)
        return carry

    lax.fori_loop(0, block_x + 5, section_one, 0)

    def section_two(x, row, fields, open_x):
        middles = [one_ref[field, x + 3, row : row + 8, :] for field in range(4)]
        taps, centre = weights(middles[:3], 0.5 * time_step, z_masks)
        values = []
        for field in fields:
            value = 0.5 * (raw_ref[field, x + 5, row : row + 8, :] + middles[field]) + moved_by(
                one_ref, field, x + 3, row, taps, centre, middles[field]
            )
            values.append(closed(value, field, open_x, row))
        return values

    for row in range(16, 48, 8):
        (below_ref[row - 16 : row - 8, :],) = section_two(-1, row, (0,), True)
    total_ref[...] = jnp.zeros((block_y, size_z), jnp.float32)

    def plane(x, carry):
        open_x = place_x * block_x + x != full_x - 1
        (line_ref[0:8, :],) = section_two(x, 8, (1,), open_x)
        for row in range(16, 48, 8):
            at = row - 16
            along_x, along_y, along_z, smoke = section_two(x, row, (0, 1, 2, 3), open_x)
            along_z = jnp.where(
                open_z,
                along_z + (time_step * buoyancy * 0.5) * (smoke + pltpu.roll(smoke, size_z - 1, 1)),
                0.0,
            )
            lifted_ref[0, x, at : at + 8, :] = along_x
            lifted_ref[1, x, at : at + 8, :] = along_y
            lifted_ref[2, x, at : at + 8, :] = along_z
            smoke_ref[x, at : at + 8, :] = smoke
            total_ref[at : at + 8, :] = total_ref[at : at + 8, :] + smoke
            line_ref[row - 8 : row, :] = along_y
            div_ref[pl.ds(pl.multiple_of(x * block_y, 8) + at, 8), :] = (
                along_x
                - below_ref[at : at + 8, :]
                + (along_y - line_ref[row - 9 : row - 1, :])
                + (along_z - pltpu.roll(along_z, 1, 1))
            )
            below_ref[at : at + 8, :] = along_x
        return carry

    lax.fori_loop(0, block_x, plane, 0)
    pack(div_ref, total_ref, table_ref, out_ref, freq_ref)


def pack(div_ref, total_ref, table_ref, out_ref, freq_ref):
    freq_ref[...] = dot(div_ref[...], table_ref[...], ((1,), (0,)))

    def one(x, carry):
        for part in range(4):
            for half in range(2):
                tile = freq_ref[
                    pl.ds(pl.multiple_of(x * block_y, 8) + part * 8, 8), half * 128 : half * 128 + 128
                ]
                out_ref[pl.ds(half * 8 * send_rows + part * 16 + x, 8, stride=send_rows), :] = (
                    swap_groups(tile)
                )
        return carry

    lax.fori_loop(0, block_x, one, 0)
    for part in range(4):
        for half in range(2):
            tile = total_ref[part * 8 : part * 8 + 8, half * 128 : half * 128 + 128]
            out_ref[pl.ds(half * 8 * send_rows + 64 + part, 8, stride=send_rows), :] = swap_groups(
                tile
            )
    for peer in range(count_x):
        out_ref[peer * send_rows + 68 : peer * send_rows + 72, :] = jnp.zeros((4, 128), jnp.float32)


def power_of(base, exponent, bits):
    result = jnp.ones_like(base)
    for bit in range(bits):
        result = jnp.where((exponent >> bit) & 1 == 1, result * base, result)
        base = base * base
    return result


def roots_of(lam):
    half = 0.5 * lam
    spread = jnp.sqrt(lam + half * half)
    rho = 1.0 / (1.0 + half + spread)
    return rho, spread


def squared(value, times):
    for _ in range(times):
        value = value * value
    return value


def forward_kernel(place_ref, got_ref, lam_ref, table_ref, local_ref, ends_ref, send_ref, before_ref, line_ref):
    place_y = place_ref[1]
    for part in range(4):
        lines = got_ref[:, part * 16 : part * 16 + 16, :].reshape(full_x, 128)
        line_ref[part * 128 : part * 128 + 128, :] = dot(lines, table_ref[...], ((0,), (0,)))
    lam = lam_ref[...]
    rho, _ = roots_of(lam)
    special = lam == 0.0
    low = jnp.zeros((chunk_z, full_x), jnp.float32)
    for y in range(block_y):
        low = low * rho + line_ref[y * 16 : y * 16 + 16, :]
        local_ref[y * 16 : y * 16 + 16, :] = low
    high = jnp.zeros((chunk_z, full_x), jnp.float32)
    for y in reversed(range(block_y)):
        high = high * rho
        rows = slice(y * 16, y * 16 + 16)
        here = local_ref[rows, :]
        local_ref[rows, :] = jnp.where(special, here, here + high)
        high = high + line_ref[rows, :]
    ends_ref[0] = low
    ends_ref[1] = high
    rho_32 = squared(rho, 5)
    rho_64 = rho_32 * rho_32
    up = low + power_of(rho_64, place_y, 4) * rho_32 * high
    down = high + power_of(rho_64, count_y - 1 - place_y, 4) * rho_32 * low
    for peer in range(count_y):
        send_ref[peer] = jnp.where(peer > place_y, up, down)
    running = jnp.zeros((4, 128), jnp.float32)
    for peer in range(count_x):
        before_ref[peer, 0:4, :] = running
        running = running + got_ref[peer, 64:68, :]


def backward_kernel(
    place_ref, local_ref, ends_ref, got_ref, lam_ref, table_ref, next_ref, before_ref, out_ref, line_ref
):
    place_y = place_ref[1]
    lam = lam_ref[...]
    rho, spread = roots_of(lam)
    special = lam == 0.0
    scale = jnp.where(special, 0.0, -0.5 / jnp.where(special, 1.0, spread))
    low, high = ends_ref[0], ends_ref[1]
    rho_32 = squared(rho, 5)
    rho_64 = rho_32 * rho_32
    rho_up = power_of(rho_64, place_y, 4)
    rho_down = power_of(rho_64, count_y - 1 - place_y, 4)
    from_low = jnp.zeros((chunk_z, full_x), jnp.float32)
    from_high = jnp.zeros((chunk_z, full_x), jnp.float32)
    for peer in range(count_y):
        from_low = jnp.where(peer < place_y, from_low * rho_32 + got_ref[peer], from_low)
        other = count_y - 1 - peer
        from_high = jnp.where(other > place_y, from_high * rho_32 + got_ref[other], from_high)
    rho_992 = rho_up * rho_down * rho_32
    wrap = 1.0 / jnp.where(special, 1.0, 1.0 - rho_992 * rho_32)
    enter_low = (from_low + rho_up * (rho_32 * from_high + high) + rho_992 * low) * wrap
    enter_high = (from_high + rho_down * (rho_32 * from_low + low) + rho_992 * high) * wrap
    mean = (0.5 * (from_low + from_high) + low) * (1.0 / full_y)
    flux_in = 0.5 * from_low - mean * (place_y * block_y).astype(jnp.float32)
    for y in reversed(range(block_y)):
        enter_high_next = enter_high
        rows = slice((y + 1) * 16, (y + 1) * 16 + 16)
        if y + 1 == block_y:
            line_ref[rows, :] = rho * low + enter_high_next
        else:
            line_ref[rows, :] = local_ref[rows, :] + jnp.where(special, 0.0, enter_high_next)
        enter_high = enter_high * rho
    line_ref[0:16, :] = local_ref[0:16, :] + jnp.where(special, 0.0, enter_high)
    level = jnp.zeros((chunk_z, full_x), jnp.float32)
    for y in range(block_y + 1):
        rows = slice(y * 16, y * 16 + 16)
        enter_low = enter_low * rho
        here = line_ref[rows, :]
        line_ref[rows, :] = jnp.where(special, level, scale * (here + enter_low))
        level = level + (here + flux_in - mean * (y + 1.0))
    line_ref[(block_y + 1) * 16 :, :] = jnp.zeros((112, full_x), jnp.float32)
    for part in range(5):
        lines = line_ref[part * 128 : part * 128 + 128, :]
        out_ref[:, part * 16 : part * 16 + 16, :] = dot(table_ref[...], lines, ((1,), (1,))).reshape(
            count_x, block_x, 128
        )
        if part < 4:
            out_ref[:, 80 + part : 81 + part, :] = dot(next_ref[...], lines, ((1,), (1,))).reshape(
                count_x, 1, 128
            )
    out_ref[:, 84:88, :] = before_ref[:, 0:4, :]


def final_kernel(place_ref, got_ref, lifted_ref, smoke_ref, table_ref, out_ref, glow_ref, freq_ref, press_ref):
    place_x, place_y = place_ref[0], place_ref[1]

    def tile_at(row, half):
        return swap_groups(got_ref[pl.ds(half * 8 * back_rows + row, 8, stride=back_rows), :])

    def one(x, carry):
        for part in range(5):
            for half in range(2):
                freq_ref[x, part * 8 : part * 8 + 8, half * 128 : half * 128 + 128] = tile_at(
                    part * 16 + x, half
                )
        return carry

    lax.fori_loop(0, block_x, one, 0)
    for part in range(4):
        for half in range(2):
            freq_ref[block_x, part * 8 : part * 8 + 8, half * 128 : half * 128 + 128] = tile_at(
                80 + part, half
            )
    freq_ref[block_x, 32:40, :] = jnp.zeros((8, size_z), jnp.float32)
    press_ref[...] = dot(
        freq_ref[...].reshape((block_x + 1) * 40, size_z), table_ref[...], ((1,), (0,))
    ).reshape(block_x + 1, 40, size_z)
    along_y = lax.broadcasted_iota(jnp.int32, (block_y, size_z), 0) + place_y * block_y
    along_z = lax.broadcasted_iota(jnp.int32, (block_y, size_z), 1)
    open_y = along_y < full_y - 1
    open_z = along_z < size_z - 1
    entered = jnp.concatenate(
        [
            jnp.concatenate([tile_at(84 + part, half) for half in range(2)], axis=1)
            for part in range(4)
        ],
        axis=0,
    )
    attenuation = extinction / full_x

    def finish(x, running):
        here = press_ref[x, 0:block_y, :]
        open_x = place_x * block_x + x < full_x - 1
        out_ref[0, x] = jnp.where(
            open_x, lifted_ref[0, x] - (press_ref[x + 1, 0:block_y, :] - here), 0.0
        )
        out_ref[1, x] = jnp.where(
            open_y, lifted_ref[1, x] - (press_ref[x, 1 : block_y + 1, :] - here), 0.0
        )
        out_ref[2, x] = jnp.where(
            open_z, lifted_ref[2, x] - (pltpu.roll(here, size_z - 1, 1) - here), 0.0
        )
        smoke = smoke_ref[x]
        depth = attenuation * smoke
        series = 1.0 - depth * (1.0 / 7.0)
        for order in (6.0, 5.0, 4.0, 3.0, 2.0):
            series = 1.0 - depth * (1.0 / order) * series
        lost = jnp.where(jnp.abs(depth) < 0.25, depth * series, 1.0 - jnp.exp(-depth))
        glow_ref[x] = jnp.exp(-attenuation * running) * lost * (1.0 / attenuation)
        return running + smoke

    lax.fori_loop(0, block_x, finish, entered)


def shaped(*dims):
    return jax.ShapeDtypeStruct(dims, jnp.float32)


def call(kernel, outs, scratch, scalars=True):
    vmem = pl.BlockSpec(memory_space=pltpu.VMEM)

    def run(*args):
        specs = [vmem] * len(args)
        if scalars:
            specs[0] = pl.BlockSpec(memory_space=pltpu.SMEM)
        return pl.pallas_call(
            kernel,
            out_shape=outs,
            in_specs=specs,
            out_specs=jax.tree.map(lambda _: vmem, outs),
            scratch_shapes=[pltpu.VMEM(dims, jnp.float32) for dims in scratch],
            name=kernel.__name__,
        )(*args)

    return run


def step(place_x, place_y, velocity, density, rims):
    place = jnp.stack([place_x, place_y]).astype(jnp.int32)
    table_z = cosine_array(size_z)
    table_x = cosine_array(full_x)
    next_x = np.concatenate(
        [table_x.T[block_x::block_x], np.zeros((1, full_x), np.float32)], axis=0
    )
    lam = (
        lax.dynamic_slice_in_dim(jnp.asarray(eigen_array(size_z)), place_x * chunk_z, chunk_z)[:, None]
        + jnp.asarray(eigen_array(full_x))[None, :]
    )
    lifted, smoke, packed = call(
        advect_kernel,
        (
            shaped(3, block_x, block_y, size_z),
            shaped(block_x, block_y, size_z),
            shaped(count_x * send_rows, 128),
        ),
        [
            (4, block_x + 9, 64, size_z),
            (4, block_x + 5, 64, size_z),
            (block_y + 8, size_z),
            (block_y, size_z),
            (block_x * block_y, size_z),
            (block_x * block_y, size_z),
            (block_y, size_z),
        ],
    )(place, velocity, density, *rims, jnp.asarray(np.ascontiguousarray(table_z.T)))
    got = lax.all_to_all(
        packed.reshape(count_x, send_rows, 128), "gx", split_axis=0, concat_axis=0, tiled=True
    )
    table_xt = jnp.asarray(np.ascontiguousarray(table_x.T))
    local, ends, moments, before = call(
        forward_kernel,
        (
            shaped(block_y * chunk_z, full_x),
            shaped(2, chunk_z, full_x),
            shaped(count_y, chunk_z, full_x),
            shaped(count_x, 8, 128),
        ),
        [(block_y * chunk_z, full_x)],
    )(place, got, lam, table_xt)
    moments = lax.all_to_all(moments, "gy", split_axis=0, concat_axis=0, tiled=True)
    back = call(
        backward_kernel,
        shaped(count_x, back_rows, 128),
        [(5 * 128, full_x)],
    )(place, local, ends, moments, lam, table_xt, jnp.asarray(next_x), before)
    back = lax.all_to_all(back, "gx", split_axis=0, concat_axis=0, tiled=True)
    return call(
        final_kernel,
        (shaped(3, block_x, block_y, size_z), shaped(block_x, block_y, size_z)),
        [(block_x + 1, 40, size_z), (block_x + 1, 40, size_z)],
    )(place, back.reshape(count_x * back_rows, 128), lifted, smoke, jnp.asarray(table_z))


def per_device(velocity, density):
    upward = [(i, i + 1) for i in range(15)]
    downward = [(i + 1, i) for i in range(15)]

    def slab(x_part, y_part):
        parts = [velocity[:, x_part, y_part], density[None, x_part, y_part]]
        return jnp.concatenate([part.astype(jnp.float32) for part in parts], axis=0)

    everything = slice(None)
    top = slab(slice(block_x - 4, None), everything).reshape(16, block_y, size_z)
    fifth = velocity[0, block_x - 5 : block_x - 4].astype(jnp.float32)
    low_x = lax.ppermute(jnp.concatenate([top, fifth], axis=0), "gx", upward)
    high_x = lax.ppermute(
        slab(slice(0, 4), everything).reshape(16, block_y, size_z), "gx", downward
    )
    low_y = lax.ppermute(slab(everything, slice(block_y - 8, None)), "gy", upward)
    high_y = lax.ppermute(slab(everything, slice(0, 8)), "gy", downward)

    def corner(x_part):
        return jnp.concatenate([low_y[:, x_part, 4:8], high_y[:, x_part, 0:4]], axis=2)

    low_c = lax.ppermute(corner(slice(block_x - 4, None)), "gx", upward)
    high_c = lax.ppermute(corner(slice(0, 4)), "gx", downward)
    return step(
        lax.axis_index("gx"),
        lax.axis_index("gy"),
        velocity,
        density,
        (low_x, high_x, low_y, high_y, low_c, high_c),
    )


def solution(mesh):
    in_specs = (P(None, "gx", "gy", None), P("gx", "gy", None))
    out_specs = (P(None, "gx", "gy", None), P("gx", "gy", None))
    return jax.shard_map(
        per_device, mesh=mesh, in_specs=in_specs, out_specs=out_specs, check_vma=False
    )
```

```python
import jax
import jax.numpy as jnp
import numpy as np
from jax import lax
from jax.experimental import pallas as pl
from jax.experimental.pallas import tpu as pltpu
from jax.sharding import PartitionSpec as P

time_step = 0.4
buoyancy = 2.0
extinction = 3.0
highest = lax.Precision.HIGHEST

block_x, block_y, size_z = 16, 32, 256
count_x, count_y = 16, 16
full_x, full_y = 256, 512
chunk_z = 16
send_rows = 72
back_rows = 88


def cosine_array(length):
    modes = np.arange(length, dtype=np.float64)[:, None]
    centres = np.arange(length, dtype=np.float64)[None, :] + 0.5
    factor = np.where(modes == 0, np.sqrt(1.0 / length), np.sqrt(2.0 / length))
    return (factor * np.cos(np.pi * modes * centres / length)).astype(np.float32)


def eigen_array(length):
    modes = np.arange(length, dtype=np.float64)
    return (4.0 * np.sin(np.pi * modes / (2 * length)) ** 2).astype(np.float32)


def swap_groups(tile):
    row = lax.broadcasted_iota(jnp.int32, (8, 128), 0)
    group = lax.broadcasted_iota(jnp.int32, (8, 128), 1) // 16
    for step in (1, 2, 4):
        row_bit = (row & step) != 0
        group_bit = (group & step) != 0
        below = pltpu.roll(pltpu.roll(tile, 8 - step, 0), 16 * step, 1)
        above = pltpu.roll(pltpu.roll(tile, step, 0), 128 - 16 * step, 1)
        tile = jnp.where(
            row_bit == group_bit, tile, jnp.where(group_bit, below, above)
        )
    return tile


def turn_groups(tile):
    row = lax.broadcasted_iota(jnp.int32, (8, 128), 0)
    group = lax.broadcasted_iota(jnp.int32, (8, 128), 1) // 16
    skewed = pltpu.roll(tile, 0, 1, stride=16, stride_axis=0)
    return pltpu.roll(
        jnp.take_along_axis(skewed, (row + group) & 7, axis=0), 0, 1, stride=16, stride_axis=0
    )


turned = [half * 128 + (-group % 8) * 16 + mode for half in range(2) for group in range(8) for mode in range(16)]


def dot(left, right, dims):
    return lax.dot_general(
        left, right, (dims, ((), ())), precision=highest, preferred_element_type=jnp.float32
    )


def weights(speeds, step, half, lane):
    taps = []
    centre = None
    for axis, speed in enumerate(speeds):
        scaled = speed * (step / 6.0)
        ahead = jnp.maximum(scaled, 0.0)
        back = ahead - scaled
        both = ahead + back
        centre = both if centre is None else centre + both
        plus_two, minus_two = back, ahead
        plus_one = 6.0 * back - 2.0 * ahead
        minus_one = 6.0 * ahead - 2.0 * back
        if axis == 2 and half == 0:
            minus_one = jnp.where(lane > 0, minus_one, 0.0)
            minus_two = jnp.where(lane > 1, minus_two, 0.0)
        if axis == 2 and half == 1:
            plus_one = jnp.where(lane < 127, plus_one, 0.0)
            plus_two = jnp.where(lane < 126, plus_two, 0.0)
        taps.append((plus_two, plus_one, minus_one, minus_two))
    return taps, -3.0 * centre


def moved_along_z(pair, half, shift, lane):
    here = pltpu.roll(pair[half], (128 - shift) % 128, 1)
    if (shift > 0) == (half == 1):
        return here
    other = pltpu.roll(pair[1 - half], (128 - shift) % 128, 1)
    return jnp.where(lane < 128 - shift if shift > 0 else lane >= -shift, here, other)


def change(ref, field, x, tile, half, pair, taps, centre, lane):
    total = centre * pair[half]
    for axis, (plus_two, plus_one, minus_one, minus_two) in enumerate(taps):
        if axis == 0:
            parts = [ref[field, x + shift, half, tile] for shift in (2, 1, -1, -2)]
        elif axis == 1:
            parts = [ref[field, x, half, tile + shift] for shift in (2, 1, -1, -2)]
        else:
            parts = [moved_along_z(pair, half, shift, lane) for shift in (2, 1, -1, -2)]
        total = total - plus_two * parts[0]
        total = total + plus_one * parts[1]
        total = total + minus_one * parts[2]
        total = total - minus_two * parts[3]
    return total


tiles = 5


def advect_kernel(
    velocity_hbm, density_hbm, low_x_ref, high_x_ref, low_y_ref, high_y_ref, low_c_ref,
    high_c_ref, table_ref, lifted_ref, smoke_ref, out_ref,
    stage_ref, raw_ref, one_ref, below_ref, div_ref, freq_ref, sum_ref, total_ref,
    velocity_ref, density_ref, arrived,
):
    copies = fetched(velocity_hbm, density_hbm, velocity_ref, density_ref, arrived)
    for copy in copies:
        copy.start()
    place_x, place_y = lax.axis_index("gx"), lax.axis_index("gy")

    def fill_rims(pair, carry):
        for field in range(4):
            for half in range(2):
                low, high = low_y_ref[field, pair, half], high_y_ref[field, pair, half]
                at = 2 * pair + 5
                stage_ref[field, at, half, 4:8, :] = low[0:4]
                stage_ref[field, at + 1, half, 4:8, :] = low[4:8]
                stage_ref[field, at, half, 40:44, :] = high[0:4]
                stage_ref[field, at + 1, half, 40:44, :] = high[4:8]
        return carry

    lax.fori_loop(0, block_x // 2, fill_rims, 0)
    for x in range(block_x):
        for half in range(2):
            stage_ref[1, x + 5, half, 3:4, :] = low_y_ref[4, x // 8, half, x % 8 : x % 8 + 1, :]
    for field in range(4):
        for x in range(4):
            for half in range(2):
                for at, edge_ref, corner_ref in ((1, low_x_ref, low_c_ref), (21, high_x_ref, high_c_ref)):
                    stage_ref[field, x + at, half, 8:40, :] = edge_ref[field * 4 + x, half]
                    corner = corner_ref[field, x, half]
                    stage_ref[field, x + at, half, 4:8, :] = corner[4:8]
                    stage_ref[field, x + at, half, 40:44, :] = corner[0:4]
    for half in range(2):
        stage_ref[0, 0, half, 8:40, :] = low_x_ref[16, half]

    for copy in copies:
        copy.wait()

    def fill(x, carry):
        for field in range(4):
            source = (velocity_ref[field, x] if field < 3 else density_ref[x]).astype(jnp.float32)
            for half in range(2):
                stage_ref[field, x + 5, half, 8:40, :] = source[:, half * 128 : half * 128 + 128]
        return carry

    lax.fori_loop(0, block_x, fill, 0)

    def spread(x, carry):
        for field in range(4):
            for half in range(2):
                for tile in range(-2, tiles + 2):
                    raw_ref[field, x, half, tile + 2] = stage_ref[
                        field, x, half, pl.ds(3 + tile, 8, stride=5), :
                    ]
        return carry

    lax.fori_loop(0, block_x + 9, spread, 0)

    lane = lax.broadcasted_iota(jnp.int32, (8, 128), 1)
    last_row = (lax.broadcasted_iota(jnp.int32, (8, 128), 0) == 7) & (place_y == count_y - 1)
    halves = range(2)

    def closed(value, field, open_x, tile, half):
        if field == 0:
            return jnp.where(open_x, value, 0.0)
        if field == 1 and tile == 1:
            return jnp.where(last_row, 0.0, value)
        if field == 2 and half == 1:
            return jnp.where(lane < 127, value, 0.0)
        return value

    def section_one(x, carry):
        open_x = place_x * block_x + x - 3 != full_x - 1
        for tile in range(tiles):
            pairs = [[raw_ref[field, x + 2, half, tile + 2] for half in halves] for field in range(4)]
            for half in halves:
                taps, centre = weights([pairs[c][half] for c in range(3)], time_step, half, lane)
                for field in range(4):
                    value = pairs[field][half] + change(
                        raw_ref, field, x + 2, tile + 2, half, pairs[field], taps, centre, lane
                    )
                    value = closed(value, field, open_x, tile, half)
                    one_ref[field, x, half, tile + 2] = value
                    if tile < 2:
                        one_ref[field, x, half, tile + 7] = pltpu.roll(value, 7, 0)
                    if tile > 2:
                        one_ref[field, x, half, tile - 3] = pltpu.roll(value, 1, 0)
        return carry

    lax.fori_loop(0, block_x + 5, section_one, 0)

    def section_two(x, tile, fields, open_x):
        pairs = [[one_ref[field, x + 3, half, tile + 2] for half in halves] for field in range(4)]
        values = {field: [] for field in fields}
        for half in halves:
            taps, centre = weights([pairs[c][half] for c in range(3)], 0.5 * time_step, half, lane)
            for field in fields:
                value = 0.5 * (raw_ref[field, x + 5, half, tile + 2] + pairs[field][half]) + change(
                    one_ref, field, x + 3, tile + 2, half, pairs[field], taps, centre, lane
                )
                values[field].append(closed(value, field, open_x, tile, half))
        return values

    for tile in range(tiles):
        for half in halves:
            sum_ref[half, tile] = jnp.zeros((8, 128), jnp.float32)
        for half, value in enumerate(section_two(-1, tile, (0,), True)[0]):
            below_ref[half, tile] = value

    def plane(x, carry):
        open_x = place_x * block_x + x != full_x - 1
        waiting, previous = None, None
        for tile in range(tiles):
            rows = pl.ds(3 + tile, 8, stride=5)
            values = section_two(x, tile, (0, 1, 2, 3), open_x)
            smoke = values[3]
            along_z = [
                values[2][half]
                + (time_step * buoyancy * 0.5)
                * (smoke[half] + moved_along_z(smoke, half, 1, lane))
                for half in halves
            ]
            along_z[1] = jnp.where(lane < 127, along_z[1], 0.0)
            div = []
            for half in halves:
                sum_ref[half, tile] = sum_ref[half, tile] + smoke[half]
                beneath = moved_along_z(along_z, half, -1, lane)
                if half == 0:
                    beneath = jnp.where(lane > 0, beneath, 0.0)
                div.append(
                    values[0][half]
                    - below_ref[half, tile]
                    + (along_z[half] - beneath)
                    + values[1][half]
                )
                below_ref[half, tile] = values[0][half]
                lifted_ref[0, x, half, rows, :] = values[0][half]
                lifted_ref[1, x, half, rows, :] = values[1][half]
                lifted_ref[2, x, half, rows, :] = along_z[half]
                smoke_ref[x, half, rows, :] = smoke[half]
                if tile > 0:
                    div_ref[x, half, rows, :] = div[half] - previous[half]
            if tile == 0:
                waiting = div
            previous = values[1]
        for half in halves:
            div_ref[x, half, pl.ds(3, 8, stride=5), :] = waiting[half] - pltpu.roll(
                previous[half], 1, 0
            )
        return carry

    lax.fori_loop(0, block_x, plane, 0)
    for tile in range(tiles):
        for half in halves:
            total_ref[half, pl.ds(3 + tile, 8, stride=5), :] = sum_ref[half, tile]
    lines = [div_ref[:, half, 8:40, :].reshape(block_x * block_y, 128) for half in halves]
    freq_ref[...] = dot(jnp.concatenate(lines, axis=1), table_ref[...], ((1,), (0,)))

    def pack(x, carry):
        for part in range(4):
            for half in halves:
                tile = freq_ref[
                    pl.ds(pl.multiple_of(x * block_y, 8) + part * 8, 8), half * 128 : half * 128 + 128
                ]
                out_ref[pl.ds(half * 8 * send_rows + part * 16 + x, 8, stride=send_rows), :] = (
                    turn_groups(tile)
                )
        return carry

    lax.fori_loop(0, block_x, pack, 0)
    for part in range(4):
        for half in halves:
            tile = total_ref[half, 8 + part * 8 : 16 + part * 8, :]
            out_ref[pl.ds(half * 8 * send_rows + 64 + part, 8, stride=send_rows), :] = swap_groups(
                tile
            )
    for peer in range(count_x):
        out_ref[peer * send_rows + 68 : peer * send_rows + 72, :] = jnp.zeros((4, 128), jnp.float32)


def edge_kernel(
    velocity_hbm, density_hbm, up_x_ref, down_x_ref, up_y_ref, down_y_ref,
    velocity_ref, density_ref, arrived,
):
    copies = fetched(velocity_hbm, density_hbm, velocity_ref, density_ref, arrived)
    for copy in copies:
        copy.start()
    for copy in copies:
        copy.wait()
    row = lax.broadcasted_iota(jnp.int32, (8, 128), 0)
    low_rows = row < 4

    def rows_of(field, x):
        return (velocity_ref[field, x] if field < 3 else density_ref[x]).astype(jnp.float32)

    for field in range(4):
        for x in range(4):
            top, bottom = rows_of(field, block_x - 4 + x), rows_of(field, x)
            for half in range(2):
                lanes = slice(half * 128, half * 128 + 128)
                up_x_ref[field * 4 + x, half] = top[:, lanes]
                down_x_ref[field * 4 + x, half] = bottom[:, lanes]
        for pair in range(block_x // 2):
            first, second = rows_of(field, 2 * pair), rows_of(field, 2 * pair + 1)
            for half in range(2):
                lanes = slice(half * 128, half * 128 + 128)
                up_y_ref[field, pair, half] = jnp.where(
                    low_rows,
                    pltpu.roll(first[block_y - 8 :, lanes], 4, 0),
                    second[block_y - 8 :, lanes],
                )
                down_y_ref[field, pair, half] = jnp.where(
                    low_rows, first[:8, lanes], pltpu.roll(second[:8, lanes], 4, 0)
                )
    for group in range(2):
        for half in range(2):
            lanes = slice(half * 128, half * 128 + 128)
            tile = jnp.zeros((8, 128), jnp.float32)
            for x in range(8):
                rows = rows_of(1, group * 8 + x)[block_y - 8 :, lanes]
                tile = jnp.where(row == x, pltpu.roll(rows, (x + 5) % 8, 0), tile)
            up_y_ref[4, group, half] = tile
    fifth = rows_of(0, block_x - 5)
    for half in range(2):
        up_x_ref[16, half] = fifth[:, half * 128 : half * 128 + 128]


def corner_kernel(low_y_ref, high_y_ref, up_ref, down_ref):
    row = lax.broadcasted_iota(jnp.int32, (8, 128), 0)
    for field in range(4):
        for x in range(4):
            for half in range(2):
                for at, ref in ((block_x - 4, up_ref), (0, down_ref)):
                    high = high_y_ref[field, (at + x) // 2, half]
                    low = low_y_ref[field, (at + x) // 2, half]
                    if x % 2 == 0:
                        low = pltpu.roll(low, 4, 0)
                    else:
                        high = pltpu.roll(high, 4, 0)
                    ref[field, x, half] = jnp.where(row < 4, high, low)


def power_of(base, exponent, bits):
    result = jnp.ones_like(base)
    for bit in range(bits):
        result = jnp.where((exponent >> bit) & 1 == 1, result * base, result)
        base = base * base
    return result


def roots_of(lam):
    half = 0.5 * lam
    spread = jnp.sqrt(lam + half * half)
    rho = 1.0 / (1.0 + half + spread)
    return rho, spread


def eigen_sum(eigen_ref, eigen_x_ref, place_x):
    row = lax.broadcasted_iota(jnp.int32, (chunk_z, full_x), 0)
    along_z = jnp.zeros((chunk_z, full_x), jnp.float32)
    for at in range(chunk_z):
        along_z = jnp.where(row == at, eigen_ref[place_x * chunk_z + at], along_z)
    return along_z + eigen_x_ref[...]


def squared(value, times):
    for _ in range(times):
        value = value * value
    return value


def forward_kernel(
    eigen_ref, got_ref, eigen_x_ref, table_ref, local_ref, ends_ref, send_ref, before_ref, line_ref
):
    place_x, place_y = lax.axis_index("gx"), lax.axis_index("gy")
    for part in range(4):
        lines = got_ref[:, part * 16 : part * 16 + 16, :].reshape(full_x, 128)
        line_ref[part * 128 : part * 128 + 128, :] = dot(lines, table_ref[...], ((0,), (0,)))
    lam = eigen_sum(eigen_ref, eigen_x_ref, place_x)
    rho, _ = roots_of(lam)
    special = lam == 0.0
    low = jnp.zeros((chunk_z, full_x), jnp.float32)
    for y in range(block_y):
        low = low * rho + line_ref[y * 16 : y * 16 + 16, :]
        local_ref[y * 16 : y * 16 + 16, :] = low
    high = jnp.zeros((chunk_z, full_x), jnp.float32)
    for y in reversed(range(block_y)):
        high = high * rho
        rows = slice(y * 16, y * 16 + 16)
        here = local_ref[rows, :]
        local_ref[rows, :] = jnp.where(special, here, here + high)
        high = high + line_ref[rows, :]
    ends_ref[0] = low
    ends_ref[1] = high
    rho_32 = squared(rho, 5)
    rho_64 = rho_32 * rho_32
    up = low + power_of(rho_64, place_y, 4) * rho_32 * high
    down = high + power_of(rho_64, count_y - 1 - place_y, 4) * rho_32 * low
    for peer in range(count_y):
        send_ref[peer] = jnp.where(peer > place_y, up, down)
    running = jnp.zeros((4, 128), jnp.float32)
    for peer in range(count_x):
        before_ref[peer, 0:4, :] = running
        running = running + got_ref[peer, 64:68, :]


def turned_rows(y):
    at = (y // 8) * 128 + (-y % 8) * 16
    return slice(at, at + 16)


def backward_kernel(
    eigen_ref, local_ref, ends_ref, got_ref, eigen_x_ref, table_ref, next_ref, before_ref, out_ref, line_ref
):
    place_x, place_y = lax.axis_index("gx"), lax.axis_index("gy")
    lam = eigen_sum(eigen_ref, eigen_x_ref, place_x)
    rho, spread = roots_of(lam)
    special = lam == 0.0
    scale = jnp.where(special, 0.0, -0.5 / jnp.where(special, 1.0, spread))
    low, high = ends_ref[0], ends_ref[1]
    rho_32 = squared(rho, 5)
    rho_64 = rho_32 * rho_32
    rho_up = power_of(rho_64, place_y, 4)
    rho_down = power_of(rho_64, count_y - 1 - place_y, 4)
    from_low = jnp.zeros((chunk_z, full_x), jnp.float32)
    from_high = jnp.zeros((chunk_z, full_x), jnp.float32)
    for peer in range(count_y):
        from_low = jnp.where(peer < place_y, from_low * rho_32 + got_ref[peer], from_low)
        other = count_y - 1 - peer
        from_high = jnp.where(other > place_y, from_high * rho_32 + got_ref[other], from_high)
    rho_992 = rho_up * rho_down * rho_32
    wrap = 1.0 / jnp.where(special, 1.0, 1.0 - rho_992 * rho_32)
    enter_low = (from_low + rho_up * (rho_32 * from_high + high) + rho_992 * low) * wrap
    enter_high = (from_high + rho_down * (rho_32 * from_low + low) + rho_992 * high) * wrap
    mean = (0.5 * (from_low + from_high) + low) * (1.0 / full_y)
    flux_in = 0.5 * from_low - mean * (place_y * block_y).astype(jnp.float32)
    for y in reversed(range(block_y)):
        enter_high_next = enter_high
        rows = slice((y + 1) * 16, (y + 1) * 16 + 16)
        if y + 1 == block_y:
            line_ref[turned_rows(y + 1), :] = rho * low + enter_high_next
        else:
            line_ref[turned_rows(y + 1), :] = local_ref[rows, :] + jnp.where(
                special, 0.0, enter_high_next
            )
        enter_high = enter_high * rho
    line_ref[0:16, :] = local_ref[0:16, :] + jnp.where(special, 0.0, enter_high)
    level = jnp.zeros((chunk_z, full_x), jnp.float32)
    for y in range(block_y + 1):
        rows = turned_rows(y)
        enter_low = enter_low * rho
        here = line_ref[rows, :]
        line_ref[rows, :] = jnp.where(special, level, scale * (here + enter_low))
        level = level + (here + flux_in - mean * (y + 1.0))
    line_ref[(block_y + 1) * 16 :, :] = jnp.zeros((112, full_x), jnp.float32)
    for part in range(5):
        lines = line_ref[part * 128 : part * 128 + 128, :]
        out_ref[:, part * 16 : part * 16 + 16, :] = dot(table_ref[...], lines, ((1,), (1,))).reshape(
            count_x, block_x, 128
        )
        if part < 4:
            out_ref[:, 80 + part : 81 + part, :] = dot(next_ref[...], lines, ((1,), (1,))).reshape(
                count_x, 1, 128
            )
    out_ref[:, 84:88, :] = before_ref[:, 0:4, :]


def final_kernel(
    got_ref, lifted_ref, smoke_ref, table_ref, out_hbm, glow_hbm,
    freq_ref, press_ref, out_ref, glow_ref, out_sent, glow_sent,
):
    place_x, place_y = lax.axis_index("gx"), lax.axis_index("gy")

    def tile_at(row, half, change=turn_groups):
        return change(got_ref[pl.ds(half * 8 * back_rows + row, 8, stride=back_rows), :])

    entered = jnp.concatenate(
        [
            jnp.concatenate([tile_at(84 + part, half, swap_groups) for half in range(2)], axis=1)
            for part in range(4)
        ],
        axis=0,
    )
    attenuation = extinction / full_x

    def whole(ref, *at):
        return jnp.concatenate([ref[(*at, half, slice(8, 40))] for half in range(2)], axis=1)

    def out_copy(x):
        return pltpu.make_async_copy(out_ref.at[x], out_hbm.at[:, x], out_sent.at[x])

    def glow_copy(x):
        return pltpu.make_async_copy(glow_ref.at[x], glow_hbm.at[x], glow_sent.at[x])

    def whole(ref, *at):
        return jnp.concatenate([ref[(*at, half, slice(8, 40))] for half in range(2)], axis=1)

    def shine(x, running):
        smoke = whole(smoke_ref, x)
        depth = attenuation * smoke
        series = 1.0 - depth * (1.0 / 7.0)
        for order in (6.0, 5.0, 4.0, 3.0, 2.0):
            series = 1.0 - depth * (1.0 / order) * series
        lost = jnp.where(jnp.abs(depth) < 0.25, depth * series, 1.0 - jnp.exp(-depth))
        glow_ref[x] = jnp.exp(-attenuation * running) * lost * (1.0 / attenuation)
        glow_copy(x).start()
        return running + smoke

    lax.fori_loop(0, block_x, shine, entered)

    def one(x, carry):
        for part in range(5):
            for half in range(2):
                freq_ref[x, part * 8 : part * 8 + 8, half * 128 : half * 128 + 128] = tile_at(
                    part * 16 + x, half
                )
        return carry

    lax.fori_loop(0, block_x, one, 0)
    for part in range(4):
        for half in range(2):
            freq_ref[block_x, part * 8 : part * 8 + 8, half * 128 : half * 128 + 128] = tile_at(
                80 + part, half
            )
    freq_ref[block_x, 32:40, :] = jnp.zeros((8, size_z), jnp.float32)
    press_ref[...] = dot(
        freq_ref[...].reshape((block_x + 1) * 40, size_z), table_ref[...], ((1,), (0,))
    ).reshape(block_x + 1, 40, size_z)
    along_y = lax.broadcasted_iota(jnp.int32, (block_y, size_z), 0) + place_y * block_y
    along_z = lax.broadcasted_iota(jnp.int32, (block_y, size_z), 1)
    open_y = along_y < full_y - 1
    open_z = along_z < size_z - 1

    def finish(x, carry):
        here = press_ref[x, 0:block_y, :]
        open_x = place_x * block_x + x < full_x - 1
        out_ref[x, 0] = jnp.where(
            open_x, whole(lifted_ref, 0, x) - (press_ref[x + 1, 0:block_y, :] - here), 0.0
        )
        out_ref[x, 1] = jnp.where(
            open_y, whole(lifted_ref, 1, x) - (press_ref[x, 1 : block_y + 1, :] - here), 0.0
        )
        out_ref[x, 2] = jnp.where(
            open_z, whole(lifted_ref, 2, x) - (pltpu.roll(here, size_z - 1, 1) - here), 0.0
        )
        out_copy(x).start()
        return carry

    lax.fori_loop(0, block_x, finish, 0)

    def drain(x, carry):
        glow_copy(x).wait()
        out_copy(x).wait()
        return carry

    lax.fori_loop(0, block_x, drain, 0)


def shaped(*dims):
    return jax.ShapeDtypeStruct(dims, jnp.float32)


def call(kernel, outs, scratch, grant, spaces={}, outside=False):
    vmem = pl.BlockSpec(memory_space=pltpu.VMEM)

    def run(*args):
        specs = [
            pl.BlockSpec(memory_space=spaces[at]) if at in spaces else vmem
            for at in range(len(args))
        ]
        place = pl.BlockSpec(memory_space=pltpu.HBM) if outside else vmem
        return pl.pallas_call(
            kernel,
            out_shape=outs,
            in_specs=specs,
            out_specs=jax.tree.map(lambda _: place, outs),
            scratch_shapes=[
                pltpu.VMEM(entry, jnp.float32) if isinstance(entry, tuple) else entry
                for entry in scratch
            ],
            compiler_params=pltpu.CompilerParams(vmem_limit_bytes=grant << 20),
            cost_estimate=pl.CostEstimate(
                flops=10**9, bytes_accessed=1024, transcendentals=0
            ),
        )(*args)

    return run


inputs_here = [
    pltpu.VMEM((3, block_x, block_y, size_z), jnp.bfloat16),
    pltpu.VMEM((block_x, block_y, size_z), jnp.bfloat16),
    pltpu.SemaphoreType.DMA((2,)),
]


def fetched(velocity_hbm, density_hbm, velocity_ref, density_ref, arrived):
    return [
        pltpu.make_async_copy(velocity_hbm, velocity_ref, arrived.at[0]),
        pltpu.make_async_copy(density_hbm, density_ref, arrived.at[1]),
    ]


def step(velocity, density, rims):
    table_z = cosine_array(size_z)
    table_x = cosine_array(full_x)
    next_x = np.concatenate(
        [table_x.T[block_x::block_x], np.zeros((1, full_x), np.float32)], axis=0
    )
    eigen_z = jnp.asarray(eigen_array(size_z))
    eigen_x = jnp.asarray(np.broadcast_to(eigen_array(full_x)[None, :], (chunk_z, full_x)))
    lifted, smoke, packed = call(
        advect_kernel,
        (
            shaped(3, block_x, 2, 48, 128),
            shaped(block_x, 2, 48, 128),
            shaped(count_x * send_rows, 128),
        ),
        [
            (4, block_x + 9, 2, 48, 128),
            (4, block_x + 9, 2, 9, 8, 128),
            (4, block_x + 5, 2, 9, 8, 128),
            (2, tiles, 8, 128),
            (block_x, 2, 48, 128),
            (block_x * block_y, size_z),
            (2, tiles, 8, 128),
            (2, 48, 128),
            *inputs_here,
        ],
        25,
        {0: pltpu.HBM, 1: pltpu.HBM},
    )(velocity, density, *rims, jnp.asarray(np.ascontiguousarray(table_z.T[:, turned])))
    got = lax.all_to_all(
        packed.reshape(count_x, send_rows, 128), "gx", split_axis=0, concat_axis=0, tiled=True
    )
    table_xt = jnp.asarray(np.ascontiguousarray(table_x.T))
    local, ends, moments, before = call(
        forward_kernel,
        (
            shaped(block_y * chunk_z, full_x),
            shaped(2, chunk_z, full_x),
            shaped(count_y, chunk_z, full_x),
            shaped(count_x, 8, 128),
        ),
        [(block_y * chunk_z, full_x)],
        4,
        {0: pltpu.SMEM},
    )(eigen_z, got, eigen_x, table_xt)
    moments = lax.all_to_all(moments, "gy", split_axis=0, concat_axis=0, tiled=True)
    back = call(
        backward_kernel,
        shaped(count_x, back_rows, 128),
        [(5 * 128, full_x)],
        4,
        {0: pltpu.SMEM},
    )(eigen_z, local, ends, moments, eigen_x, table_xt, jnp.asarray(next_x), before)
    back = lax.all_to_all(back, "gx", split_axis=0, concat_axis=0, tiled=True)
    return call(
        final_kernel,
        (shaped(3, block_x, block_y, size_z), shaped(block_x, block_y, size_z)),
        [
            (block_x + 1, 40, size_z),
            (block_x + 1, 40, size_z),
            (block_x, 3, block_y, size_z),
            (block_x, block_y, size_z),
            pltpu.SemaphoreType.DMA((block_x,)),
            pltpu.SemaphoreType.DMA((block_x,)),
        ],
        8,
        outside=True,
    )(back.reshape(count_x * back_rows, 128), lifted, smoke, jnp.asarray(table_z))


def moved(part, axis, upward):
    pairs = [(i, i + 1) if upward else (i + 1, i) for i in range(15)]
    return lax.ppermute(part, axis, pairs)


def per_device(velocity, density):
    planes, rows = (2, block_y, 128), (block_x // 2, 2, 8, 128)
    up_x, down_x, up_y, down_y = call(
        edge_kernel,
        (shaped(17, *planes), shaped(16, *planes), shaped(5, *rows), shaped(4, *rows)),
        inputs_here,
        4,
        {0: pltpu.HBM, 1: pltpu.HBM},
    )(velocity, density)
    low_x = moved(up_x, "gx", True)
    high_x = moved(down_x, "gx", False)
    low_y = moved(up_y, "gy", True)
    high_y = moved(down_y, "gy", False)
    corner = shaped(4, 4, 2, 8, 128)
    up_c, down_c = call(corner_kernel, (corner, corner), [], 2)(low_y, high_y)
    low_c = moved(up_c, "gx", True)
    high_c = moved(down_c, "gx", False)
    return step(velocity, density, (low_x, high_x, low_y, high_y, low_c, high_c))


def solution(mesh):
    in_specs = (P(None, "gx", "gy", None), P("gx", "gy", None))
    out_specs = (P(None, "gx", "gy", None), P("gx", "gy", None))
    return jax.shard_map(
        per_device, mesh=mesh, in_specs=in_specs, out_specs=out_specs, check_vma=False
    )
```

```python
import functools

import jax
import jax.numpy as jnp
import numpy as np
from jax import lax
from jax.experimental import pallas as pl
from jax.experimental.pallas import tpu as pltpu
from jax.sharding import PartitionSpec as P

time_step = 0.4
buoyancy = 2.0
extinction = 3.0
highest = lax.Precision.HIGHEST

block_x, block_y, size_z = 16, 32, 256
count_x, count_y = 16, 16
full_x, full_y = 256, 512
chunk_z = 16
send_rows = 72
back_rows = 88


def cosine_array(length):
    modes = np.arange(length, dtype=np.float64)[:, None]
    centres = np.arange(length, dtype=np.float64)[None, :] + 0.5
    factor = np.where(modes == 0, np.sqrt(1.0 / length), np.sqrt(2.0 / length))
    return (factor * np.cos(np.pi * modes * centres / length)).astype(np.float32)


def eigen_array(length):
    modes = np.arange(length, dtype=np.float64)
    return (4.0 * np.sin(np.pi * modes / (2 * length)) ** 2).astype(np.float32)


def swap_groups(tile):
    row = lax.broadcasted_iota(jnp.int32, (8, 128), 0)
    group = lax.broadcasted_iota(jnp.int32, (8, 128), 1) // 16
    skewed = pltpu.roll(tile, 0, 1, stride=16, stride_axis=0)
    upturned = pltpu.roll(
        jnp.take_along_axis(skewed, (row + group + 1) & 7, axis=0), 16, 1, stride=16, stride_axis=0
    )
    return jnp.take_along_axis(upturned, 7 - row, axis=0)


def turn_groups(tile):
    row = lax.broadcasted_iota(jnp.int32, (8, 128), 0)
    group = lax.broadcasted_iota(jnp.int32, (8, 128), 1) // 16
    skewed = pltpu.roll(tile, 0, 1, stride=16, stride_axis=0)
    return pltpu.roll(
        jnp.take_along_axis(skewed, (row + group) & 7, axis=0), 0, 1, stride=16, stride_axis=0
    )


turned = [half * 128 + (-group % 8) * 16 + mode for half in range(2) for group in range(8) for mode in range(16)]


def dot(left, right, dims):
    return lax.dot_general(
        left, right, (dims, ((), ())), precision=highest, preferred_element_type=jnp.float32
    )


def weights(speeds, step, half, lane):
    taps = []
    centre = None
    for axis, speed in enumerate(speeds):
        scaled = speed * (step / 6.0)
        ahead = jnp.maximum(scaled, 0.0)
        back = ahead - scaled
        both = ahead + back
        centre = both if centre is None else centre + both
        plus_two, minus_two = back, ahead
        plus_one = 6.0 * back - 2.0 * ahead
        minus_one = 6.0 * ahead - 2.0 * back
        if axis == 2 and half == 0:
            minus_one = jnp.where(lane > 0, minus_one, 0.0)
            minus_two = jnp.where(lane > 1, minus_two, 0.0)
        if axis == 2 and half == 1:
            plus_one = jnp.where(lane < 127, plus_one, 0.0)
            plus_two = jnp.where(lane < 126, plus_two, 0.0)
        taps.append((plus_two, plus_one, minus_one, minus_two))
    return taps, -3.0 * centre


def moved_along_z(pair, half, shift, lane):
    here = pltpu.roll(pair[half], (128 - shift) % 128, 1)
    if (shift > 0) == (half == 1):
        return here
    other = pltpu.roll(pair[1 - half], (128 - shift) % 128, 1)
    return jnp.where(lane < 128 - shift if shift > 0 else lane >= -shift, here, other)


def change(ref, field, x, tile, half, pair, taps, centre, lane):
    total = centre * pair[half]
    for axis, (plus_two, plus_one, minus_one, minus_two) in enumerate(taps):
        if axis == 0:
            parts = [ref[field, x + shift, half, tile] for shift in (2, 1, -1, -2)]
        elif axis == 1:
            parts = [ref[field, x, half, tile + shift] for shift in (2, 1, -1, -2)]
        else:
            parts = [moved_along_z(pair, half, shift, lane) for shift in (2, 1, -1, -2)]
        total = total - plus_two * parts[0]
        total = total + plus_one * parts[1]
        total = total + minus_one * parts[2]
        total = total - minus_two * parts[3]
    return total


tiles = 5
halves = range(2)


def rows_of_tile(tile):
    return pl.ds(3 + tile, 8, stride=5)


def stencil(raw_ref, raw_first, one_ref, one_first):
    place_x, place_y = lax.axis_index("gx"), lax.axis_index("gy")
    lane = lax.broadcasted_iota(jnp.int32, (8, 128), 1)
    last_row = (lax.broadcasted_iota(jnp.int32, (8, 128), 0) == 7) & (place_y == count_y - 1)

    def closed(value, field, open_x, tile, half):
        if field == 0:
            return jnp.where(open_x, value, 0.0)
        if field == 1 and tile == 1:
            return jnp.where(last_row, 0.0, value)
        if field == 2 and half == 1:
            return jnp.where(lane < 127, value, 0.0)
        return value

    def is_open(x):
        return place_x * block_x + x != full_x - 1

    def section_one(x, fields=(0, 1, 2, 3)):
        at = x - raw_first
        for tile in range(tiles):
            pairs = [[raw_ref[field, at, half, tile + 2] for half in halves] for field in range(4)]
            for half in halves:
                taps, centre = weights([pairs[c][half] for c in range(3)], time_step, half, lane)
                for field in fields:
                    value = pairs[field][half] + change(
                        raw_ref, field, at, tile + 2, half, pairs[field], taps, centre, lane
                    )
                    value = closed(value, field, is_open(x), tile, half)
                    one_ref[field, x - one_first, half, tile + 2] = value
                    if tile < 2:
                        one_ref[field, x - one_first, half, tile + 7] = pltpu.roll(value, 7, 0)
                    if tile > 2:
                        one_ref[field, x - one_first, half, tile - 3] = pltpu.roll(value, 1, 0)

    def section_two(x, tile, fields):
        at = x - one_first
        pairs = [[one_ref[field, at, half, tile + 2] for half in halves] for field in range(4)]
        values = {field: [] for field in fields}
        for half in halves:
            taps, centre = weights([pairs[c][half] for c in range(3)], 0.5 * time_step, half, lane)
            for field in fields:
                value = 0.5 * (
                    raw_ref[field, x - raw_first, half, tile + 2] + pairs[field][half]
                ) + change(one_ref, field, at, tile + 2, half, pairs[field], taps, centre, lane)
                values[field].append(closed(value, field, is_open(x), tile, half))
        return values

    def plane(x, at, div_at, lifted_ref, smoke_ref, div_ref, ends_ref, hold_ref):
        for tile in range(tiles):
            values = section_two(x, tile, (0, 1, 2, 3))
            for field in range(4):
                for half in halves:
                    hold_ref[field, half, tile] = values[field][half]
        for tile in range(tiles):
            rows = rows_of_tile(tile)
            along_x, along_y, along_z, smoke = (
                [hold_ref[field, half, tile] for half in halves] for field in range(4)
            )
            along_z = [
                along_z[half]
                + (time_step * buoyancy * 0.5)
                * (smoke[half] + moved_along_z(smoke, half, 1, lane))
                for half in halves
            ]
            along_z[1] = jnp.where(lane < 127, along_z[1], 0.0)
            for half in halves:
                ends_ref[1, half, tile] = ends_ref[1, half, tile] + smoke[half]
                beneath = moved_along_z(along_z, half, -1, lane)
                if half == 0:
                    beneath = jnp.where(lane > 0, beneath, 0.0)
                below_y = hold_ref[1, half, (tile - 1) % tiles]
                if tile == 0:
                    below_y = pltpu.roll(below_y, 1, 0)
                div_ref[div_at, half, rows, :] = (
                    along_x[half]
                    - ends_ref[0, half, tile]
                    + (along_z[half] - beneath)
                    + (along_y[half] - below_y)
                )
                ends_ref[0, half, tile] = along_x[half]
                lifted_ref[0, at, half, rows, :] = along_x[half]
                lifted_ref[1, at, half, rows, :] = along_y[half]
                lifted_ref[2, at, half, rows, :] = along_z[half]
                smoke_ref[at, half, rows, :] = smoke[half]

    return section_one, section_two, plane


def fill_plane(stage_ref, at, velocity_ref, density_ref, x):
    for field in range(4):
        source = (velocity_ref[field, x] if field < 3 else density_ref[x]).astype(jnp.float32)
        for half in halves:
            stage_ref[field, at, half, 8:40, :] = source[:, half * 128 : half * 128 + 128]


def fill_rims(stage_ref, at, low_y_ref, high_y_ref, pair):
    for field in range(4):
        for half in halves:
            low, high = low_y_ref[field, pair, half], high_y_ref[field, pair, half]
            stage_ref[field, at, half, 4:8, :] = low[0:4]
            stage_ref[field, at + 1, half, 4:8, :] = low[4:8]
            stage_ref[field, at, half, 40:44, :] = high[0:4]
            stage_ref[field, at + 1, half, 40:44, :] = high[4:8]


def fill_fifth(stage_ref, at, low_y_ref, x):
    for half in halves:
        stage_ref[1, at, half, 3:4, :] = low_y_ref[4, x // 8, half, x % 8 : x % 8 + 1, :]


def spread(stage_ref, raw_ref, x):
    for field in range(4):
        for half in halves:
            for tile in range(-2, tiles + 2):
                raw_ref[field, x, half, tile + 2] = stage_ref[field, x, half, rows_of_tile(tile), :]


def each(first, last, work):
    def one(x, carry):
        work(x)
        return carry

    lax.fori_loop(first, last, one, 0)


def inner_kernel(
    velocity_hbm, density_hbm, low_y_ref, high_y_ref, one_hbm, lifted_hbm, smoke_hbm, div_hbm, ends_ref,
    stage_ref, raw_ref, one_ref, lifted_ref, smoke_ref, div_ref, hold_ref, one_sent, plane_sent,
    velocity_ref, density_ref, arrived,
):
    copies = fetched(velocity_hbm, density_hbm, velocity_ref, density_ref, arrived)
    for copy in copies:
        copy.start()
    each(0, 8, lambda pair: fill_rims(stage_ref, 2 * pair, low_y_ref, high_y_ref, pair))
    for x in range(block_x):
        fill_fifth(stage_ref, x, low_y_ref, x)
    for copy in copies:
        copy.wait()
    each(0, block_x, lambda x: fill_plane(stage_ref, x, velocity_ref, density_ref, x))
    each(0, block_x, lambda x: spread(stage_ref, raw_ref, x))
    section_one, _, plane = stencil(raw_ref, 0, one_ref, 2)
    each(2, 14, section_one)
    one_copies = [
        pltpu.make_async_copy(
            one_ref.at[:, 8 * part : 8 * part + 4], one_hbm.at[:, 4 * part : 4 * part + 4], one_sent.at[part]
        )
        for part in range(2)
    ]
    for copy in one_copies:
        copy.start()
    ends_ref[...] = jnp.zeros((2, 2, tiles, 8, 128), jnp.float32)

    def plane_copies(at):
        return (
            pltpu.make_async_copy(lifted_ref.at[:, at], lifted_hbm.at[:, at], plane_sent.at[0, at]),
            pltpu.make_async_copy(smoke_ref.at[at], smoke_hbm.at[at], plane_sent.at[1, at]),
            pltpu.make_async_copy(div_ref.at[at], div_hbm.at[at], plane_sent.at[2, at]),
        )

    def work(at):
        plane(at + 4, at, at, lifted_ref, smoke_ref, div_ref, ends_ref, hold_ref)
        for copy in plane_copies(at):
            copy.start()

    each(0, 8, work)

    def drain(at):
        for copy in plane_copies(at):
            copy.wait()

    each(0, 8, drain)
    for copy in one_copies:
        copy.wait()


def outer_kernel(
    velocity_hbm, density_hbm, one_hbm, div_hbm, inner_ends_ref, low_x_ref, high_x_ref, low_y_ref,
    high_y_ref, low_c_ref, high_c_ref, table_ref, lifted_ref, smoke_ref, out_ref,
    stage_ref, raw_ref, one_ref, ends_ref, div_ref, freq_ref, total_ref, hold_ref, one_arrived,
    velocity_ref, density_ref, arrived,
):
    copies = fetched(velocity_hbm, density_hbm, velocity_ref, density_ref, arrived)
    inner_copies = [
        pltpu.make_async_copy(
            one_hbm.at[:, 4 * part : 4 * part + 4],
            one_ref.at[:, 5 + 8 * part : 9 + 8 * part],
            one_arrived.at[part],
        )
        for part in range(2)
    ] + [pltpu.make_async_copy(div_hbm, div_ref.at[4:12], one_arrived.at[2])]
    for copy in copies + inner_copies:
        copy.start()
    for field in range(4):
        for x in range(4):
            for half in halves:
                for at, edge_ref, corner_ref in ((1, low_x_ref, low_c_ref), (21, high_x_ref, high_c_ref)):
                    stage_ref[field, x + at, half, 8:40, :] = edge_ref[field * 4 + x, half]
                    corner = corner_ref[field, x, half]
                    stage_ref[field, x + at, half, 4:8, :] = corner[4:8]
                    stage_ref[field, x + at, half, 40:44, :] = corner[0:4]
    for half in halves:
        stage_ref[0, 0, half, 8:40, :] = low_x_ref[16, half]
    for pair in (0, 1, 6, 7):
        fill_rims(stage_ref, 2 * pair + 5, low_y_ref, high_y_ref, pair)
    for x in (0, 1, 2, 3, 12, 13, 14, 15):
        fill_fifth(stage_ref, x + 5, low_y_ref, x)
    for copy in copies:
        copy.wait()

    def fill(at):
        x = jnp.where(at < 4, at, at + 8)
        fill_plane(stage_ref, x + 5, velocity_ref, density_ref, x)

    each(0, 8, fill)
    section_one, section_two, plane = stencil(raw_ref, -5, one_ref, -3)

    each(0, 17, lambda at: spread(stage_ref, raw_ref, jnp.where(at < 9, at, at + 8)))
    section_one(-3, (0,))
    each(0, 8, lambda at: section_one(jnp.where(at < 4, at - 2, at + 10)))
    for copy in inner_copies:
        copy.wait()
    for tile in range(tiles):
        for half, value in enumerate(section_two(-1, tile, (0,))[0]):
            ends_ref[0, half, tile] = value
    ends_ref[1] = inner_ends_ref[1]
    each(0, 4, lambda x: plane(x, x, x, lifted_ref, smoke_ref, div_ref, ends_ref, hold_ref))
    for tile in range(tiles):
        for half in halves:
            rows = rows_of_tile(tile)
            div_ref[4, half, rows, :] = div_ref[4, half, rows, :] - ends_ref[0, half, tile]
    ends_ref[0] = inner_ends_ref[0]
    each(12, 16, lambda x: plane(x, x - 8, x, lifted_ref, smoke_ref, div_ref, ends_ref, hold_ref))
    for tile in range(tiles):
        for half in halves:
            total_ref[half, rows_of_tile(tile), :] = ends_ref[1, half, tile]
    lines = [div_ref[:, half, 8:40, :].reshape(block_x * block_y, 128) for half in halves]
    freq_ref[...] = dot(jnp.concatenate(lines, axis=1), table_ref[...], ((1,), (0,)))

    def pack(step):
        for x in range(4):
            x = step * 4 + x
            for part in range(4):
                for half in halves:
                    tile = freq_ref[
                        pl.ds(pl.multiple_of(x * block_y, 8) + part * 8, 8),
                        half * 128 : half * 128 + 128,
                    ]
                    out_ref[
                        pl.ds(half * 8 * send_rows + part * 16 + x, 8, stride=send_rows), :
                    ] = turn_groups(tile)

    each(0, block_x // 4, pack)
    for part in range(4):
        for half in halves:
            tile = total_ref[half, 8 + part * 8 : 16 + part * 8, :]
            out_ref[pl.ds(half * 8 * send_rows + 64 + part, 8, stride=send_rows), :] = swap_groups(
                tile
            )
    for peer in range(count_x):
        out_ref[peer * send_rows + 68 : peer * send_rows + 72, :] = jnp.zeros((4, 128), jnp.float32)


def edge_kernel(
    velocity_hbm, density_hbm, up_x_ref, down_x_ref, up_y_ref, down_y_ref,
    velocity_ref, density_ref, arrived,
):
    copies = fetched(velocity_hbm, density_hbm, velocity_ref, density_ref, arrived)
    for copy in copies:
        copy.start()
    for copy in copies:
        copy.wait()
    row = lax.broadcasted_iota(jnp.int32, (8, 128), 0)
    low_rows = row < 4

    def rows_of(field, x):
        return (velocity_ref[field, x] if field < 3 else density_ref[x]).astype(jnp.float32)

    for field in range(4):
        for x in range(4):
            top, bottom = rows_of(field, block_x - 4 + x), rows_of(field, x)
            for half in range(2):
                lanes = slice(half * 128, half * 128 + 128)
                up_x_ref[field * 4 + x, half] = top[:, lanes]
                down_x_ref[field * 4 + x, half] = bottom[:, lanes]
        for pair in range(block_x // 2):
            first, second = rows_of(field, 2 * pair), rows_of(field, 2 * pair + 1)
            for half in range(2):
                lanes = slice(half * 128, half * 128 + 128)
                up_y_ref[field, pair, half] = jnp.where(
                    low_rows,
                    pltpu.roll(first[block_y - 8 :, lanes], 4, 0),
                    second[block_y - 8 :, lanes],
                )
                down_y_ref[field, pair, half] = jnp.where(
                    low_rows, first[:8, lanes], pltpu.roll(second[:8, lanes], 4, 0)
                )
    for group in range(2):
        for half in range(2):
            lanes = slice(half * 128, half * 128 + 128)
            tile = jnp.zeros((8, 128), jnp.float32)
            for x in range(8):
                rows = rows_of(1, group * 8 + x)[block_y - 8 :, lanes]
                tile = jnp.where(row == x, pltpu.roll(rows, (x + 5) % 8, 0), tile)
            up_y_ref[4, group, half] = tile
    fifth = rows_of(0, block_x - 5)
    for half in range(2):
        up_x_ref[16, half] = fifth[:, half * 128 : half * 128 + 128]


def corner_kernel(low_y_ref, high_y_ref, up_ref, down_ref):
    row = lax.broadcasted_iota(jnp.int32, (8, 128), 0)
    for field in range(4):
        for x in range(4):
            for half in range(2):
                for at, ref in ((block_x - 4, up_ref), (0, down_ref)):
                    high = high_y_ref[field, (at + x) // 2, half]
                    low = low_y_ref[field, (at + x) // 2, half]
                    if x % 2 == 0:
                        low = pltpu.roll(low, 4, 0)
                    else:
                        high = pltpu.roll(high, 4, 0)
                    ref[field, x, half] = jnp.where(row < 4, high, low)


def power_of(base, exponent, bits):
    result = jnp.ones_like(base)
    for bit in range(bits):
        result = jnp.where((exponent >> bit) & 1 == 1, result * base, result)
        base = base * base
    return result


def roots_of(lam):
    half = 0.5 * lam
    spread = jnp.sqrt(lam + half * half)
    rho = 1.0 / (1.0 + half + spread)
    return rho, spread


def eigen_sum(eigen_ref, eigen_x_ref, place_x):
    row = lax.broadcasted_iota(jnp.int32, (chunk_z, full_x), 0)
    along_z = jnp.zeros((chunk_z, full_x), jnp.float32)
    for at in range(chunk_z):
        along_z = jnp.where(row == at, eigen_ref[place_x * chunk_z + at], along_z)
    return along_z + eigen_x_ref[...]


def squared(value, times):
    for _ in range(times):
        value = value * value
    return value


def forward_kernel(
    eigen_ref, got_ref, eigen_x_ref, table_ref, local_ref, ends_ref, send_ref, before_ref, line_ref
):
    place_x, place_y = lax.axis_index("gx"), lax.axis_index("gy")
    lines = [got_ref[:, part * 16 : part * 16 + 16, :].reshape(full_x, 128) for part in range(4)]
    line_ref[...] = dot(jnp.concatenate(lines, axis=1), table_ref[...], ((0,), (0,)))
    lam = eigen_sum(eigen_ref, eigen_x_ref, place_x)
    rho, _ = roots_of(lam)
    special = lam == 0.0
    low = jnp.zeros((chunk_z, full_x), jnp.float32)
    for y in range(block_y):
        low = low * rho + line_ref[y * 16 : y * 16 + 16, :]
        local_ref[y * 16 : y * 16 + 16, :] = low
    high = jnp.zeros((chunk_z, full_x), jnp.float32)
    for y in reversed(range(block_y)):
        high = high * rho
        rows = slice(y * 16, y * 16 + 16)
        here = local_ref[rows, :]
        local_ref[rows, :] = jnp.where(special, here, here + high)
        high = high + line_ref[rows, :]
    ends_ref[0] = low
    ends_ref[1] = high
    rho_32 = squared(rho, 5)
    rho_64 = rho_32 * rho_32
    up = low + power_of(rho_64, place_y, 4) * rho_32 * high
    down = high + power_of(rho_64, count_y - 1 - place_y, 4) * rho_32 * low
    for peer in range(count_y):
        send_ref[peer] = jnp.where(peer > place_y, up, down)
    running = jnp.zeros((4, 128), jnp.float32)
    for peer in range(count_x):
        before_ref[peer, 0:4, :] = running
        running = running + got_ref[peer, 64:68, :]


def turned_rows(y):
    at = (y // 8) * 128 + (-y % 8) * 16
    return slice(at, at + 16)


def backward_kernel(
    eigen_ref, local_ref, ends_ref, got_ref, eigen_x_ref, table_ref, before_ref, out_ref, line_ref
):
    place_x, place_y = lax.axis_index("gx"), lax.axis_index("gy")
    lam = eigen_sum(eigen_ref, eigen_x_ref, place_x)
    rho, spread = roots_of(lam)
    special = lam == 0.0
    scale = jnp.where(special, 0.0, -0.5 / jnp.where(special, 1.0, spread))
    low, high = ends_ref[0], ends_ref[1]
    rho_32 = squared(rho, 5)
    rho_64 = rho_32 * rho_32
    rho_up = power_of(rho_64, place_y, 4)
    rho_down = power_of(rho_64, count_y - 1 - place_y, 4)
    from_low = jnp.zeros((chunk_z, full_x), jnp.float32)
    from_high = jnp.zeros((chunk_z, full_x), jnp.float32)
    for peer in range(count_y):
        from_low = jnp.where(peer < place_y, from_low * rho_32 + got_ref[peer], from_low)
        other = count_y - 1 - peer
        from_high = jnp.where(other > place_y, from_high * rho_32 + got_ref[other], from_high)
    rho_992 = rho_up * rho_down * rho_32
    wrap = 1.0 / jnp.where(special, 1.0, 1.0 - rho_992 * rho_32)
    enter_low = (from_low + rho_up * (rho_32 * from_high + high) + rho_992 * low) * wrap
    enter_high = (from_high + rho_down * (rho_32 * from_low + low) + rho_992 * high) * wrap
    mean = (0.5 * (from_low + from_high) + low) * (1.0 / full_y)
    flux_in = 0.5 * from_low - mean * (place_y * block_y).astype(jnp.float32)
    for y in reversed(range(block_y)):
        enter_high_next = enter_high
        rows = slice((y + 1) * 16, (y + 1) * 16 + 16)
        if y + 1 == block_y:
            line_ref[turned_rows(y + 1), :] = rho * low + enter_high_next
        else:
            line_ref[turned_rows(y + 1), :] = local_ref[rows, :] + jnp.where(
                special, 0.0, enter_high_next
            )
        enter_high = enter_high * rho
    line_ref[0:16, :] = local_ref[0:16, :] + jnp.where(special, 0.0, enter_high)
    level = jnp.zeros((chunk_z, full_x), jnp.float32)
    for y in range(block_y + 1):
        rows = turned_rows(y)
        enter_low = enter_low * rho
        here = line_ref[rows, :]
        line_ref[rows, :] = jnp.where(special, level, scale * (here + enter_low))
        level = level + (here + flux_in - mean * (y + 1.0))
    line_ref[(block_y + 1) * 16 :, :] = jnp.zeros((112, full_x), jnp.float32)
    found = dot(table_ref[...], line_ref[...], ((1,), (1,)))
    for part in range(5):
        lanes = slice(part * 128, part * 128 + 128)
        out_ref[:, part * 16 : part * 16 + 16, :] = found[:, lanes].reshape(count_x, block_x, 128)
        if part < 4:
            for peer in range(count_x - 1):
                at = (peer + 1) * block_x
                out_ref[peer, 80 + part : 81 + part, :] = found[at : at + 1, lanes]
            out_ref[count_x - 1, 80 + part : 81 + part, :] = jnp.zeros((1, 128), jnp.float32)
    out_ref[:, 84:88, :] = before_ref[:, 0:4, :]


def final_kernel(
    got_ref, lifted_ref, lifted_in_ref, smoke_ref, smoke_in_ref, table_ref, out_hbm, glow_hbm,
    freq_ref, press_ref, out_ref, glow_ref, out_sent, glow_sent,
):
    place_x, place_y = lax.axis_index("gx"), lax.axis_index("gy")

    def tile_at(row, half, change=turn_groups):
        return change(got_ref[pl.ds(half * 8 * back_rows + row, 8, stride=back_rows), :])

    entered = jnp.concatenate(
        [
            jnp.concatenate([tile_at(84 + part, half, swap_groups) for half in range(2)], axis=1)
            for part in range(4)
        ],
        axis=0,
    )
    attenuation = extinction / full_x

    def whole(ref, *at):
        return jnp.concatenate([ref[(*at, half, slice(8, 40))] for half in range(2)], axis=1)

    def out_copy(x):
        return pltpu.make_async_copy(out_ref.at[x], out_hbm.at[:, x], out_sent.at[x])

    def glow_copy(x):
        return pltpu.make_async_copy(glow_ref.at[x], glow_hbm.at[x], glow_sent.at[x])

    def whole(ref, *at):
        return jnp.concatenate([ref[(*at, half, slice(8, 40))] for half in range(2)], axis=1)

    def shine(ref, shift, x, running):
        smoke = whole(ref, x - shift)
        depth = attenuation * smoke
        series = 1.0 - depth * (1.0 / 7.0)
        for order in (6.0, 5.0, 4.0, 3.0, 2.0):
            series = 1.0 - depth * (1.0 / order) * series
        lost = jnp.where(jnp.abs(depth) < 0.25, depth * series, 1.0 - jnp.exp(-depth))
        glow_ref[x] = jnp.exp(-attenuation * running) * lost * (1.0 / attenuation)
        glow_copy(x).start()
        return running + smoke

    parts = ((0, 4, 0, lifted_ref, smoke_ref), (4, 12, 4, lifted_in_ref, smoke_in_ref),
             (12, 16, 8, lifted_ref, smoke_ref))
    for first, last, shift, _, ref in parts:
        entered = lax.fori_loop(first, last, functools.partial(shine, ref, shift), entered)

    def unpack(step):
        for x in range(4):
            x = step * 4 + x
            for part in range(5):
                for half in range(2):
                    freq_ref[x, part * 8 : part * 8 + 8, half * 128 : half * 128 + 128] = tile_at(
                        part * 16 + x, half
                    )

    each(0, block_x // 4, unpack)
    for part in range(4):
        for half in range(2):
            freq_ref[block_x, part * 8 : part * 8 + 8, half * 128 : half * 128 + 128] = tile_at(
                80 + part, half
            )
    freq_ref[block_x, 32:40, :] = jnp.zeros((8, size_z), jnp.float32)
    press_ref[...] = dot(
        freq_ref[...].reshape((block_x + 1) * 40, size_z), table_ref[...], ((1,), (0,))
    ).reshape(block_x + 1, 40, size_z)
    along_y = lax.broadcasted_iota(jnp.int32, (block_y, size_z), 0) + place_y * block_y
    along_z = lax.broadcasted_iota(jnp.int32, (block_y, size_z), 1)
    open_y = along_y < full_y - 1
    open_z = along_z < size_z - 1

    def finish(ref, shift, first):
        for x in range(first, first + 4):
            here = press_ref[x, 0:block_y, :]
            open_x = place_x * block_x + x < full_x - 1
            out_ref[x, 0] = jnp.where(
                open_x, whole(ref, 0, x - shift) - (press_ref[x + 1, 0:block_y, :] - here), 0.0
            )
            out_ref[x, 1] = jnp.where(
                open_y, whole(ref, 1, x - shift) - (press_ref[x, 1 : block_y + 1, :] - here), 0.0
            )
            out_ref[x, 2] = jnp.where(
                open_z, whole(ref, 2, x - shift) - (pltpu.roll(here, size_z - 1, 1) - here), 0.0
            )
        for x in range(first, first + 4):
            out_copy(x).start()

    for first, ref, shift in (
        (0, lifted_ref, 0),
        (4, lifted_in_ref, 4),
        (8, lifted_in_ref, 4),
        (12, lifted_ref, 8),
    ):
        finish(ref, shift, first)

    def drain(x, carry):
        glow_copy(x).wait()
        out_copy(x).wait()
        return carry

    lax.fori_loop(0, block_x, drain, 0)


def shaped(*dims):
    return jax.ShapeDtypeStruct(dims, jnp.float32)


def call(kernel, outs, scratch, grant, spaces={}, outside=0):
    vmem = pl.BlockSpec(memory_space=pltpu.VMEM)

    def run(*args):
        specs = [
            pl.BlockSpec(memory_space=spaces[at]) if at in spaces else vmem
            for at in range(len(args))
        ]
        places = [
            pl.BlockSpec(memory_space=pltpu.HBM) if at < outside else vmem
            for at in range(len(jax.tree.leaves(outs)))
        ]
        return pl.pallas_call(
            kernel,
            out_shape=outs,
            in_specs=specs,
            out_specs=jax.tree.unflatten(jax.tree.structure(outs), places),
            scratch_shapes=[
                pltpu.VMEM(entry, jnp.float32) if isinstance(entry, tuple) else entry
                for entry in scratch
            ],
            compiler_params=pltpu.CompilerParams(vmem_limit_bytes=grant << 20),
            cost_estimate=pl.CostEstimate(
                flops=10**9, bytes_accessed=1024, transcendentals=0
            ),
        )(*args)

    return run


inputs_here = [
    pltpu.VMEM((3, block_x, block_y, size_z), jnp.bfloat16),
    pltpu.VMEM((block_x, block_y, size_z), jnp.bfloat16),
    pltpu.SemaphoreType.DMA((2,)),
]


def fetched(velocity_hbm, density_hbm, velocity_ref, density_ref, arrived):
    return [
        pltpu.make_async_copy(velocity_hbm, velocity_ref, arrived.at[0]),
        pltpu.make_async_copy(density_hbm, density_ref, arrived.at[1]),
    ]


def step(velocity, density, rims):
    table_z = cosine_array(size_z)
    table_x = cosine_array(full_x)
    eigen_z = jnp.asarray(eigen_array(size_z))
    eigen_x = jnp.asarray(np.broadcast_to(eigen_array(full_x)[None, :], (chunk_z, full_x)))
    low_x, high_x, low_y, high_y, low_c, high_c = rims
    here = {0: pltpu.HBM, 1: pltpu.HBM, 2: pltpu.HBM, 3: pltpu.HBM}
    thick, plane = (2, 9, 8, 128), (2, 48, 128)
    one, lifted_in, smoke_in, div_in, ends = call(
        inner_kernel,
        (
            shaped(4, 8, *thick),
            shaped(3, 8, *plane),
            shaped(8, *plane),
            shaped(8, *plane),
            shaped(2, 2, tiles, 8, 128),
        ),
        [
            (4, block_x, *plane),
            (4, block_x, *thick),
            (4, 12, *thick),
            (3, 8, *plane),
            (8, *plane),
            (8, *plane),
            (4, 2, tiles, 8, 128),
            pltpu.SemaphoreType.DMA((2,)),
            pltpu.SemaphoreType.DMA((3, 8)),
            *inputs_here,
        ],
        20,
        {0: pltpu.HBM, 1: pltpu.HBM},
        outside=4,
    )(velocity, density, low_y, high_y)
    lifted, smoke, packed = call(
        outer_kernel,
        (shaped(3, 8, *plane), shaped(8, *plane), shaped(count_x * send_rows, 128)),
        [
            (4, block_x + 9, *plane),
            (4, block_x + 9, *thick),
            (4, block_x + 5, *thick),
            (2, 2, tiles, 8, 128),
            (block_x, *plane),
            (block_x * block_y, size_z),
            plane,
            (4, 2, tiles, 8, 128),
            pltpu.SemaphoreType.DMA((3,)),
            *inputs_here,
        ],
        25,
        here,
    )(
        velocity, density, one, div_in, ends, low_x, high_x, low_y, high_y, low_c, high_c,
        jnp.asarray(np.ascontiguousarray(table_z.T[:, turned])),
    )
    got = lax.all_to_all(
        packed.reshape(count_x, send_rows, 128), "gx", split_axis=0, concat_axis=0, tiled=True
    )
    table_xt = jnp.asarray(np.ascontiguousarray(table_x.T))
    local, ends, moments, before = call(
        forward_kernel,
        (
            shaped(block_y * chunk_z, full_x),
            shaped(2, chunk_z, full_x),
            shaped(count_y, chunk_z, full_x),
            shaped(count_x, 8, 128),
        ),
        [(block_y * chunk_z, full_x)],
        4,
        {0: pltpu.SMEM},
    )(eigen_z, got, eigen_x, table_xt)
    moments = lax.all_to_all(moments, "gy", split_axis=0, concat_axis=0, tiled=True)
    back = call(
        backward_kernel,
        shaped(count_x, back_rows, 128),
        [(5 * 128, full_x)],
        4,
        {0: pltpu.SMEM},
    )(eigen_z, local, ends, moments, eigen_x, table_xt, before)
    back = lax.all_to_all(back, "gx", split_axis=0, concat_axis=0, tiled=True)
    return call(
        final_kernel,
        (shaped(3, block_x, block_y, size_z), shaped(block_x, block_y, size_z)),
        [
            (block_x + 1, 40, size_z),
            (block_x + 1, 40, size_z),
            (block_x, 3, block_y, size_z),
            (block_x, block_y, size_z),
            pltpu.SemaphoreType.DMA((block_x,)),
            pltpu.SemaphoreType.DMA((block_x,)),
        ],
        8,
        outside=2,
    )(
        back.reshape(count_x * back_rows, 128), lifted, lifted_in, smoke, smoke_in,
        jnp.asarray(table_z),
    )


def moved(part, axis, upward):
    pairs = [(i, i + 1) if upward else (i + 1, i) for i in range(15)]
    return lax.ppermute(part, axis, pairs)


def per_device(velocity, density):
    planes, rows = (2, block_y, 128), (block_x // 2, 2, 8, 128)
    up_x, down_x, up_y, down_y = call(
        edge_kernel,
        (shaped(17, *planes), shaped(16, *planes), shaped(5, *rows), shaped(4, *rows)),
        inputs_here,
        4,
        {0: pltpu.HBM, 1: pltpu.HBM},
    )(
        pltpu.with_memory_space_constraint(velocity, pltpu.HBM),
        pltpu.with_memory_space_constraint(density, pltpu.HBM),
    )
    low_x = moved(up_x, "gx", True)
    high_x = moved(down_x, "gx", False)
    low_y = moved(up_y, "gy", True)
    high_y = moved(down_y, "gy", False)
    corner = shaped(4, 4, 2, 8, 128)
    up_c, down_c = call(corner_kernel, (corner, corner), [], 2)(low_y, high_y)
    low_c = moved(up_c, "gx", True)
    high_c = moved(down_c, "gx", False)
    return step(velocity, density, (low_x, high_x, low_y, high_y, low_c, high_c))


def solution(mesh):
    in_specs = (P(None, "gx", "gy", None), P("gx", "gy", None))
    out_specs = (P(None, "gx", "gy", None), P("gx", "gy", None))
    return jax.shard_map(
        per_device, mesh=mesh, in_specs=in_specs, out_specs=out_specs, check_vma=False
    )
```

```python
import functools

import jax
import jax.numpy as jnp
import numpy as np
from jax import lax
from jax.experimental import pallas as pl
from jax.experimental.pallas import tpu as pltpu
from jax.sharding import PartitionSpec as P

time_step = 0.4
buoyancy = 2.0
extinction = 3.0

block_x, block_y, size_z = 16, 32, 256
count_x, count_y = 16, 16
full_x, full_y = 256, 512
chunk_z = 16
send_rows = 72
back_rows = 88


def cosine_array(length):
    modes = np.arange(length, dtype=np.float64)[:, None]
    centres = np.arange(length, dtype=np.float64)[None, :] + 0.5
    factor = np.where(modes == 0, np.sqrt(1.0 / length), np.sqrt(2.0 / length))
    return (factor * np.cos(np.pi * modes * centres / length)).astype(np.float32)


def eigen_array(length):
    modes = np.arange(length, dtype=np.float64)
    return (4.0 * np.sin(np.pi * modes / (2 * length)) ** 2).astype(np.float32)


def swap_groups(tile):
    row = lax.broadcasted_iota(jnp.int32, (8, 128), 0)
    group = lax.broadcasted_iota(jnp.int32, (8, 128), 1) // 16
    skewed = pltpu.roll(tile, 0, 1, stride=16, stride_axis=0)
    upturned = pltpu.roll(
        jnp.take_along_axis(skewed, (row + group + 1) & 7, axis=0), 16, 1, stride=16, stride_axis=0
    )
    return jnp.take_along_axis(upturned, 7 - row, axis=0)


def turn_groups(tile):
    row = lax.broadcasted_iota(jnp.int32, (8, 128), 0)
    group = lax.broadcasted_iota(jnp.int32, (8, 128), 1) // 16
    skewed = pltpu.roll(tile, 0, 1, stride=16, stride_axis=0)
    return pltpu.roll(
        jnp.take_along_axis(skewed, (row + group) & 7, axis=0), 0, 1, stride=16, stride_axis=0
    )


turned = [half * 128 + (-group % 8) * 16 + mode for half in range(2) for group in range(8) for mode in range(16)]


def parts_of(value, count):
    found = []
    for _ in range(count):
        found.append(value.astype(jnp.bfloat16))
        value = value - found[-1].astype(np.float32)
    return found


pairs_of = {2: ((0, 0), (0, 1), (1, 0)), 3: ((0, 0), (0, 1), (1, 0), (0, 2), (2, 0), (1, 1))}


def data_side(value, axis, count):
    found = parts_of(value, count)
    return jnp.concatenate([found[at] for at, _ in pairs_of[count]], axis=axis)


def table_side(table, axis, count):
    found = parts_of(table, count)
    return jnp.asarray(np.concatenate([found[at] for _, at in pairs_of[count]], axis=axis))


def dot(left, right, dims):
    return lax.dot_general(left, right, (dims, ((), ())), preferred_element_type=jnp.float32)


def weights(speeds, step, half, lane):
    taps = []
    centre = None
    for axis, speed in enumerate(speeds):
        scaled = speed * (step / 6.0)
        ahead = jnp.maximum(scaled, 0.0)
        back = ahead - scaled
        both = ahead + back
        centre = both if centre is None else centre + both
        plus_two, minus_two = back, ahead
        plus_one = 6.0 * back - 2.0 * ahead
        minus_one = 6.0 * ahead - 2.0 * back
        if axis == 2 and half == 0:
            minus_one = jnp.where(lane > 0, minus_one, 0.0)
            minus_two = jnp.where(lane > 1, minus_two, 0.0)
        if axis == 2 and half == 1:
            plus_one = jnp.where(lane < 127, plus_one, 0.0)
            plus_two = jnp.where(lane < 126, plus_two, 0.0)
        taps.append((plus_two, plus_one, minus_one, minus_two))
    return taps, -3.0 * centre


def moved_along_z(pair, half, shift, lane):
    here = pltpu.roll(pair[half], (128 - shift) % 128, 1)
    if (shift > 0) == (half == 1):
        return here
    other = pltpu.roll(pair[1 - half], (128 - shift) % 128, 1)
    return jnp.where(lane < 128 - shift if shift > 0 else lane >= -shift, here, other)


def change(ref, field, x, tile, half, pair, taps, centre, lane):
    total = centre * pair[half]
    for axis, (plus_two, plus_one, minus_one, minus_two) in enumerate(taps):
        if axis == 0:
            parts = [ref[field, x + shift, half, tile] for shift in (2, 1, -1, -2)]
        elif axis == 1:
            parts = [ref[field, x, half, tile + shift] for shift in (2, 1, -1, -2)]
        else:
            parts = [moved_along_z(pair, half, shift, lane) for shift in (2, 1, -1, -2)]
        total = total - plus_two * parts[0]
        total = total + plus_one * parts[1]
        total = total + minus_one * parts[2]
        total = total - minus_two * parts[3]
    return total


tiles = 5
halves = range(2)


def rows_of_tile(tile):
    return pl.ds(3 + tile, 8, stride=5)


def stencil(raw_ref, raw_first, one_ref, one_first):
    place_x, place_y = lax.axis_index("gx"), lax.axis_index("gy")
    lane = lax.broadcasted_iota(jnp.int32, (8, 128), 1)
    last_row = (lax.broadcasted_iota(jnp.int32, (8, 128), 0) == 7) & (place_y == count_y - 1)

    def closed(value, field, open_x, tile, half):
        if field == 0:
            return jnp.where(open_x, value, 0.0)
        if field == 1 and tile == 1:
            return jnp.where(last_row, 0.0, value)
        if field == 2 and half == 1:
            return jnp.where(lane < 127, value, 0.0)
        return value

    def is_open(x):
        return place_x * block_x + x != full_x - 1

    def section_one(x, fields=(0, 1, 2, 3)):
        at = x - raw_first
        for tile in range(tiles):
            pairs = [[raw_ref[field, at, half, tile + 2] for half in halves] for field in range(4)]
            for half in halves:
                taps, centre = weights([pairs[c][half] for c in range(3)], time_step, half, lane)
                for field in fields:
                    value = pairs[field][half] + change(
                        raw_ref, field, at, tile + 2, half, pairs[field], taps, centre, lane
                    )
                    value = closed(value, field, is_open(x), tile, half)
                    one_ref[field, x - one_first, half, tile + 2] = value
                    if tile < 2:
                        one_ref[field, x - one_first, half, tile + 7] = pltpu.roll(value, 7, 0)
                    if tile > 2:
                        one_ref[field, x - one_first, half, tile - 3] = pltpu.roll(value, 1, 0)

    def section_two(x, tile, fields):
        at = x - one_first
        pairs = [[one_ref[field, at, half, tile + 2] for half in halves] for field in range(4)]
        values = {field: [] for field in fields}
        for half in halves:
            taps, centre = weights([pairs[c][half] for c in range(3)], 0.5 * time_step, half, lane)
            for field in fields:
                value = 0.5 * (
                    raw_ref[field, x - raw_first, half, tile + 2] + pairs[field][half]
                ) + change(one_ref, field, at, tile + 2, half, pairs[field], taps, centre, lane)
                values[field].append(closed(value, field, is_open(x), tile, half))
        return values

    def plane(x, at, div_at, lifted_ref, smoke_ref, div_ref, ends_ref, hold_ref):
        for tile in range(tiles):
            values = section_two(x, tile, (0, 1, 2, 3))
            for field in range(4):
                for half in halves:
                    hold_ref[field, half, tile] = values[field][half]
        for tile in range(tiles):
            rows = rows_of_tile(tile)
            along_x, along_y, along_z, smoke = (
                [hold_ref[field, half, tile] for half in halves] for field in range(4)
            )
            along_z = [
                along_z[half]
                + (time_step * buoyancy * 0.5)
                * (smoke[half] + moved_along_z(smoke, half, 1, lane))
                for half in halves
            ]
            along_z[1] = jnp.where(lane < 127, along_z[1], 0.0)
            for half in halves:
                ends_ref[1, half, tile] = ends_ref[1, half, tile] + smoke[half]
                beneath = moved_along_z(along_z, half, -1, lane)
                if half == 0:
                    beneath = jnp.where(lane > 0, beneath, 0.0)
                below_y = hold_ref[1, half, (tile - 1) % tiles]
                if tile == 0:
                    below_y = pltpu.roll(below_y, 1, 0)
                div_ref[div_at, half, rows, :] = (
                    along_x[half]
                    - ends_ref[0, half, tile]
                    + (along_z[half] - beneath)
                    + (along_y[half] - below_y)
                )
                ends_ref[0, half, tile] = along_x[half]
                lifted_ref[0, at, half, rows, :] = along_x[half]
                lifted_ref[1, at, half, rows, :] = along_y[half]
                lifted_ref[2, at, half, rows, :] = along_z[half]
                smoke_ref[at, half, rows, :] = smoke[half]

    return section_one, section_two, plane


def fill_plane(stage_ref, at, velocity_ref, density_ref, x):
    for field in range(4):
        source = (velocity_ref[field, x] if field < 3 else density_ref[x]).astype(jnp.float32)
        for half in halves:
            stage_ref[field, at, half, 8:40, :] = source[:, half * 128 : half * 128 + 128]


def fill_rims(stage_ref, at, low_y_ref, high_y_ref, pair):
    for field in range(4):
        for half in halves:
            low, high = low_y_ref[field, pair, half], high_y_ref[field, pair, half]
            stage_ref[field, at, half, 4:8, :] = low[0:4]
            stage_ref[field, at + 1, half, 4:8, :] = low[4:8]
            stage_ref[field, at, half, 40:44, :] = high[0:4]
            stage_ref[field, at + 1, half, 40:44, :] = high[4:8]


def fill_fifth(stage_ref, at, low_y_ref, x):
    for half in halves:
        stage_ref[1, at, half, 3:4, :] = low_y_ref[4, x // 8, half, x % 8 : x % 8 + 1, :]


def spread(stage_ref, raw_ref, x):
    for field in range(4):
        for half in halves:
            for tile in range(-2, tiles + 2):
                raw_ref[field, x, half, tile + 2] = stage_ref[field, x, half, rows_of_tile(tile), :]


def each(first, last, work):
    def one(x, carry):
        work(x)
        return carry

    lax.fori_loop(first, last, one, 0)


def inner_kernel(
    velocity_hbm, density_hbm, low_y_ref, high_y_ref, one_hbm, lifted_hbm, smoke_hbm, div_hbm, ends_ref,
    stage_ref, raw_ref, one_ref, lifted_ref, smoke_ref, div_ref, hold_ref, one_sent, plane_sent,
    velocity_ref, density_ref, arrived,
):
    copies = fetched(velocity_hbm, density_hbm, velocity_ref, density_ref, arrived)
    for copy in copies:
        copy.start()
    each(0, 8, lambda pair: fill_rims(stage_ref, 2 * pair, low_y_ref, high_y_ref, pair))
    for x in range(block_x):
        fill_fifth(stage_ref, x, low_y_ref, x)
    for copy in copies:
        copy.wait()
    each(0, block_x, lambda x: fill_plane(stage_ref, x, velocity_ref, density_ref, x))
    each(0, block_x, lambda x: spread(stage_ref, raw_ref, x))
    section_one, _, plane = stencil(raw_ref, 0, one_ref, 2)
    each(2, 14, section_one)
    one_copies = [
        pltpu.make_async_copy(
            one_ref.at[:, 8 * part : 8 * part + 4], one_hbm.at[:, 4 * part : 4 * part + 4], one_sent.at[part]
        )
        for part in range(2)
    ]
    for copy in one_copies:
        copy.start()
    ends_ref[...] = jnp.zeros((2, 2, tiles, 8, 128), jnp.float32)

    def plane_copies(at):
        return (
            pltpu.make_async_copy(lifted_ref.at[:, at], lifted_hbm.at[:, at], plane_sent.at[0, at]),
            pltpu.make_async_copy(smoke_ref.at[at], smoke_hbm.at[at], plane_sent.at[1, at]),
            pltpu.make_async_copy(div_ref.at[at], div_hbm.at[at], plane_sent.at[2, at]),
        )

    def work(at):
        plane(at + 4, at, at, lifted_ref, smoke_ref, div_ref, ends_ref, hold_ref)
        for copy in plane_copies(at):
            copy.start()

    each(0, 8, work)

    def drain(at):
        for copy in plane_copies(at):
            copy.wait()

    each(0, 8, drain)
    for copy in one_copies:
        copy.wait()


def outer_kernel(
    velocity_hbm, density_hbm, one_hbm, div_hbm, inner_ends_ref, low_x_ref, high_x_ref, low_y_ref,
    high_y_ref, low_c_ref, high_c_ref, table_ref, lifted_ref, smoke_ref, out_ref,
    stage_ref, raw_ref, one_ref, ends_ref, div_ref, freq_ref, total_ref, hold_ref, one_arrived,
    velocity_ref, density_ref, arrived,
):
    copies = fetched(velocity_hbm, density_hbm, velocity_ref, density_ref, arrived)
    inner_copies = [
        pltpu.make_async_copy(
            one_hbm.at[:, 4 * part : 4 * part + 4],
            one_ref.at[:, 5 + 8 * part : 9 + 8 * part],
            one_arrived.at[part],
        )
        for part in range(2)
    ] + [pltpu.make_async_copy(div_hbm, div_ref.at[4:12], one_arrived.at[2])]
    for copy in copies + inner_copies:
        copy.start()
    for field in range(4):
        for x in range(4):
            for half in halves:
                for at, edge_ref in ((1, low_x_ref), (21, high_x_ref)):
                    stage_ref[field, x + at, half, 8:40, :] = edge_ref[field * 4 + x, half]
    for at, (field, planes) in enumerate(corner_tiles):
        for half in halves:
            for corner_ref, low in ((low_c_ref, True), (high_c_ref, False)):
                corner = corner_ref[at, half]
                for place, far in enumerate(planes):
                    x = 5 - far if low else 20 + far
                    if len(planes) == 1:
                        stage_ref[field, x, half, 4:8, :] = corner[4:8]
                        stage_ref[field, x, half, 40:44, :] = corner[0:4]
                    else:
                        stage_ref[field, x, half, 6:8, :] = corner[4 * place + 2 : 4 * place + 4]
                        stage_ref[field, x, half, 40:42, :] = corner[4 * place : 4 * place + 2]
    for half in halves:
        stage_ref[0, 0, half, 8:40, :] = low_x_ref[16, half]
    for pair in (0, 1, 6, 7):
        fill_rims(stage_ref, 2 * pair + 5, low_y_ref, high_y_ref, pair)
    for x in (0, 1, 2, 3, 12, 13, 14, 15):
        fill_fifth(stage_ref, x + 5, low_y_ref, x)
    for copy in copies:
        copy.wait()

    def fill(at):
        x = jnp.where(at < 4, at, at + 8)
        fill_plane(stage_ref, x + 5, velocity_ref, density_ref, x)

    each(0, 8, fill)
    section_one, section_two, plane = stencil(raw_ref, -5, one_ref, -3)

    each(0, 17, lambda at: spread(stage_ref, raw_ref, jnp.where(at < 9, at, at + 8)))
    section_one(-3, (0,))
    each(0, 8, lambda at: section_one(jnp.where(at < 4, at - 2, at + 10)))
    for copy in inner_copies:
        copy.wait()
    for tile in range(tiles):
        for half, value in enumerate(section_two(-1, tile, (0,))[0]):
            ends_ref[0, half, tile] = value
    ends_ref[1] = inner_ends_ref[1]
    each(0, 4, lambda x: plane(x, x, x, lifted_ref, smoke_ref, div_ref, ends_ref, hold_ref))
    for tile in range(tiles):
        for half in halves:
            rows = rows_of_tile(tile)
            div_ref[4, half, rows, :] = div_ref[4, half, rows, :] - ends_ref[0, half, tile]
    ends_ref[0] = inner_ends_ref[0]
    each(12, 16, lambda x: plane(x, x - 8, x, lifted_ref, smoke_ref, div_ref, ends_ref, hold_ref))
    for tile in range(tiles):
        for half in halves:
            total_ref[half, rows_of_tile(tile), :] = ends_ref[1, half, tile]
    lines = [div_ref[:, half, 8:40, :].reshape(block_x * block_y, 128) for half in halves]
    freq_ref[...] = dot(data_side(jnp.concatenate(lines, axis=1), 1, 2), table_ref[...], ((1,), (0,)))

    def pack(step):
        for x in range(4):
            x = step * 4 + x
            for part in range(4):
                for half in halves:
                    tile = freq_ref[
                        pl.ds(pl.multiple_of(x * block_y, 8) + part * 8, 8),
                        half * 128 : half * 128 + 128,
                    ]
                    out_ref[
                        pl.ds(half * 8 * send_rows + part * 16 + x, 8, stride=send_rows), :
                    ] = turn_groups(tile)

    each(0, block_x // 4, pack)
    for part in range(4):
        for half in halves:
            tile = total_ref[half, 8 + part * 8 : 16 + part * 8, :]
            out_ref[pl.ds(half * 8 * send_rows + 64 + part, 8, stride=send_rows), :] = swap_groups(
                tile
            )
    for peer in range(count_x):
        out_ref[peer * send_rows + 68 : peer * send_rows + 72, :] = jnp.zeros((4, 128), jnp.float32)


def edge_kernel(
    velocity_hbm, density_hbm, up_x_ref, down_x_ref, up_y_ref, down_y_ref,
    velocity_ref, density_ref, arrived,
):
    copies = fetched(velocity_hbm, density_hbm, velocity_ref, density_ref, arrived)
    for copy in copies:
        copy.start()
    for copy in copies:
        copy.wait()
    row = lax.broadcasted_iota(jnp.int32, (8, 128), 0)
    low_rows = row < 4

    def rows_of(field, x):
        return (velocity_ref[field, x] if field < 3 else density_ref[x]).astype(jnp.float32)

    for field in range(4):
        for x in range(4):
            top, bottom = rows_of(field, block_x - 4 + x), rows_of(field, x)
            for half in range(2):
                lanes = slice(half * 128, half * 128 + 128)
                up_x_ref[field * 4 + x, half] = top[:, lanes]
                down_x_ref[field * 4 + x, half] = bottom[:, lanes]
        for pair in range(block_x // 2):
            first, second = rows_of(field, 2 * pair), rows_of(field, 2 * pair + 1)
            for half in range(2):
                lanes = slice(half * 128, half * 128 + 128)
                up_y_ref[field, pair, half] = jnp.where(
                    low_rows,
                    pltpu.roll(first[block_y - 8 :, lanes], 4, 0),
                    second[block_y - 8 :, lanes],
                )
                down_y_ref[field, pair, half] = jnp.where(
                    low_rows, first[:8, lanes], pltpu.roll(second[:8, lanes], 4, 0)
                )
    for group in range(2):
        for half in range(2):
            lanes = slice(half * 128, half * 128 + 128)
            tile = jnp.zeros((8, 128), jnp.float32)
            for x in range(8):
                rows = rows_of(1, group * 8 + x)[block_y - 8 :, lanes]
                tile = jnp.where(row == x, pltpu.roll(rows, (x + 5) % 8, 0), tile)
            up_y_ref[4, group, half] = tile
    fifth = rows_of(0, block_x - 5)
    for half in range(2):
        up_x_ref[16, half] = fifth[:, half * 128 : half * 128 + 128]


corner_tiles = (
    (0, (1,)), (0, (2, 3)), (1, (1,)), (1, (2,)), (1, (3, 4)), (2, (1, 2)), (3, (1, 2)),
)


def corner_kernel(low_y_ref, high_y_ref, up_ref, down_ref):
    row = lax.broadcasted_iota(jnp.int32, (8, 128), 0)

    def rows_at(field, x, half):
        low, high = low_y_ref[field, x // 2, half], high_y_ref[field, x // 2, half]
        if x % 2 == 0:
            low = pltpu.roll(low, 4, 0)
        else:
            high = pltpu.roll(high, 4, 0)
        return jnp.where(row < 4, high, low)

    for at, (field, planes) in enumerate(corner_tiles):
        for half in halves:
            for ref, upward in ((up_ref, True), (down_ref, False)):
                found = [
                    rows_at(field, block_x - far if upward else far - 1, half) for far in planes
                ]
                if len(found) == 1:
                    ref[at, half] = found[0]
                else:
                    near, far = found
                    ref[at, half] = jnp.where(
                        row < 4,
                        jnp.where(row < 2, near, pltpu.roll(near, 4, 0)),
                        jnp.where(row < 6, pltpu.roll(far, 4, 0), far),
                    )


def power_of(base, exponent, bits):
    result = jnp.ones_like(base)
    for bit in range(bits):
        result = jnp.where((exponent >> bit) & 1 == 1, result * base, result)
        base = base * base
    return result


def roots_of(lam):
    half = 0.5 * lam
    spread = jnp.sqrt(lam + half * half)
    rho = 1.0 / (1.0 + half + spread)
    return rho, spread


def eigen_sum(eigen_ref, eigen_x_ref, place_x):
    row = lax.broadcasted_iota(jnp.int32, (chunk_z, full_x), 0)
    along_z = jnp.zeros((chunk_z, full_x), jnp.float32)
    for at in range(chunk_z):
        along_z = jnp.where(row == at, eigen_ref[place_x * chunk_z + at], along_z)
    return along_z + eigen_x_ref[...]


def squared(value, times):
    for _ in range(times):
        value = value * value
    return value


def forward_kernel(
    eigen_ref, got_ref, eigen_x_ref, table_ref, local_ref, ends_ref, send_ref, before_ref, line_ref
):
    place_x, place_y = lax.axis_index("gx"), lax.axis_index("gy")
    lines = [got_ref[:, part * 16 : part * 16 + 16, :].reshape(full_x, 128) for part in range(4)]
    line_ref[...] = dot(data_side(jnp.concatenate(lines, axis=1), 0, 2), table_ref[...], ((0,), (0,)))
    lam = eigen_sum(eigen_ref, eigen_x_ref, place_x)
    rho, _ = roots_of(lam)
    special = lam == 0.0
    low = jnp.zeros((chunk_z, full_x), jnp.float32)
    for y in range(block_y):
        low = low * rho + line_ref[y * 16 : y * 16 + 16, :]
        local_ref[y * 16 : y * 16 + 16, :] = low
    high = jnp.zeros((chunk_z, full_x), jnp.float32)
    for y in reversed(range(block_y)):
        high = high * rho
        rows = slice(y * 16, y * 16 + 16)
        here = local_ref[rows, :]
        local_ref[rows, :] = jnp.where(special, here, here + high)
        high = high + line_ref[rows, :]
    ends_ref[0] = low
    ends_ref[1] = high
    rho_32 = squared(rho, 5)
    rho_64 = rho_32 * rho_32
    up = low + power_of(rho_64, place_y, 4) * rho_32 * high
    down = high + power_of(rho_64, count_y - 1 - place_y, 4) * rho_32 * low
    for peer in range(count_y):
        send_ref[peer] = jnp.where(peer > place_y, up, down)
    running = jnp.zeros((4, 128), jnp.float32)
    for peer in range(count_x):
        before_ref[peer, 0:4, :] = running
        running = running + got_ref[peer, 64:68, :]


def turned_rows(y):
    at = (y // 8) * 128 + (-y % 8) * 16
    return slice(at, at + 16)


def backward_kernel(
    eigen_ref, local_ref, ends_ref, got_ref, eigen_x_ref, table_ref, before_ref, out_ref, line_ref
):
    place_x, place_y = lax.axis_index("gx"), lax.axis_index("gy")
    lam = eigen_sum(eigen_ref, eigen_x_ref, place_x)
    rho, spread = roots_of(lam)
    special = lam == 0.0
    scale = jnp.where(special, 0.0, -0.5 / jnp.where(special, 1.0, spread))
    low, high = ends_ref[0], ends_ref[1]
    rho_32 = squared(rho, 5)
    rho_64 = rho_32 * rho_32
    rho_up = power_of(rho_64, place_y, 4)
    rho_down = power_of(rho_64, count_y - 1 - place_y, 4)
    from_low = jnp.zeros((chunk_z, full_x), jnp.float32)
    from_high = jnp.zeros((chunk_z, full_x), jnp.float32)
    for peer in range(count_y):
        from_low = jnp.where(peer < place_y, from_low * rho_32 + got_ref[peer], from_low)
        other = count_y - 1 - peer
        from_high = jnp.where(other > place_y, from_high * rho_32 + got_ref[other], from_high)
    rho_992 = rho_up * rho_down * rho_32
    wrap = 1.0 / jnp.where(special, 1.0, 1.0 - rho_992 * rho_32)
    enter_low = (from_low + rho_up * (rho_32 * from_high + high) + rho_992 * low) * wrap
    enter_high = (from_high + rho_down * (rho_32 * from_low + low) + rho_992 * high) * wrap
    mean = (0.5 * (from_low + from_high) + low) * (1.0 / full_y)
    flux_in = 0.5 * from_low - mean * (place_y * block_y).astype(jnp.float32)
    for y in reversed(range(block_y)):
        enter_high_next = enter_high
        rows = slice((y + 1) * 16, (y + 1) * 16 + 16)
        if y + 1 == block_y:
            line_ref[turned_rows(y + 1), :] = rho * low + enter_high_next
        else:
            line_ref[turned_rows(y + 1), :] = local_ref[rows, :] + jnp.where(
                special, 0.0, enter_high_next
            )
        enter_high = enter_high * rho
    line_ref[0:16, :] = local_ref[0:16, :] + jnp.where(special, 0.0, enter_high)
    level = jnp.zeros((chunk_z, full_x), jnp.float32)
    for y in range(block_y + 1):
        rows = turned_rows(y)
        enter_low = enter_low * rho
        here = line_ref[rows, :]
        line_ref[rows, :] = jnp.where(special, level, scale * (here + enter_low))
        level = level + (here + flux_in - mean * (y + 1.0))
    line_ref[(block_y + 1) * 16 :, :] = jnp.zeros((112, full_x), jnp.float32)
    found = dot(table_ref[...], data_side(line_ref[...], 1, 3), ((1,), (1,)))
    for part in range(5):
        lanes = slice(part * 128, part * 128 + 128)
        out_ref[:, part * 16 : part * 16 + 16, :] = found[:, lanes].reshape(count_x, block_x, 128)
        if part < 4:
            for peer in range(count_x - 1):
                at = (peer + 1) * block_x
                out_ref[peer, 80 + part : 81 + part, :] = found[at : at + 1, lanes]
            out_ref[count_x - 1, 80 + part : 81 + part, :] = jnp.zeros((1, 128), jnp.float32)
    out_ref[:, 84:88, :] = before_ref[:, 0:4, :]


def final_kernel(
    got_ref, lifted_ref, lifted_in_ref, smoke_ref, smoke_in_ref, table_ref, out_hbm, glow_hbm,
    freq_ref, press_ref, out_ref, glow_ref, out_sent, glow_sent,
):
    place_x, place_y = lax.axis_index("gx"), lax.axis_index("gy")

    def tile_at(row, half, change=turn_groups):
        return change(got_ref[pl.ds(half * 8 * back_rows + row, 8, stride=back_rows), :])

    entered = jnp.concatenate(
        [
            jnp.concatenate([tile_at(84 + part, half, swap_groups) for half in range(2)], axis=1)
            for part in range(4)
        ],
        axis=0,
    )
    attenuation = extinction / full_x

    def whole(ref, *at):
        return jnp.concatenate([ref[(*at, half, slice(8, 40))] for half in range(2)], axis=1)

    def out_copy(x):
        return pltpu.make_async_copy(out_ref.at[x], out_hbm.at[:, x], out_sent.at[x])

    def glow_copy(x):
        return pltpu.make_async_copy(glow_ref.at[x], glow_hbm.at[x], glow_sent.at[x])

    def whole(ref, *at):
        return jnp.concatenate([ref[(*at, half, slice(8, 40))] for half in range(2)], axis=1)

    def shine(ref, shift, x, running):
        smoke = whole(ref, x - shift)
        depth = attenuation * smoke
        series = 1.0 - depth * (1.0 / 5.0)
        for order in (4.0, 3.0, 2.0):
            series = 1.0 - depth * (1.0 / order) * series
        lost = jnp.where(jnp.abs(depth) < 0.0625, depth * series, 1.0 - jnp.exp(-depth))
        glow_ref[x] = jnp.exp(-attenuation * running) * lost * (1.0 / attenuation)
        glow_copy(x).start()
        return running + smoke

    parts = ((0, 4, 0, lifted_ref, smoke_ref), (4, 12, 4, lifted_in_ref, smoke_in_ref),
             (12, 16, 8, lifted_ref, smoke_ref))
    for first, last, shift, _, ref in parts:
        entered = lax.fori_loop(first, last, functools.partial(shine, ref, shift), entered)

    def unpack(step):
        for x in range(4):
            x = step * 4 + x
            for part in range(5):
                for half in range(2):
                    freq_ref[x, part * 8 : part * 8 + 8, half * 128 : half * 128 + 128] = tile_at(
                        part * 16 + x, half
                    )

    each(0, block_x // 4, unpack)
    for part in range(4):
        for half in range(2):
            freq_ref[block_x, part * 8 : part * 8 + 8, half * 128 : half * 128 + 128] = tile_at(
                80 + part, half
            )
    freq_ref[block_x, 32:40, :] = jnp.zeros((8, size_z), jnp.float32)
    press_ref[...] = dot(
        data_side(freq_ref[...].reshape((block_x + 1) * 40, size_z), 1, 3), table_ref[...], ((1,), (0,))
    ).reshape(block_x + 1, 40, size_z)
    along_y = lax.broadcasted_iota(jnp.int32, (block_y, size_z), 0) + place_y * block_y
    along_z = lax.broadcasted_iota(jnp.int32, (block_y, size_z), 1)
    open_y = along_y < full_y - 1
    open_z = along_z < size_z - 1

    def finish(ref, shift, first):
        for x in range(first, first + 4):
            here = press_ref[x, 0:block_y, :]
            open_x = place_x * block_x + x < full_x - 1
            out_ref[x, 0] = jnp.where(
                open_x, whole(ref, 0, x - shift) - (press_ref[x + 1, 0:block_y, :] - here), 0.0
            )
            out_ref[x, 1] = jnp.where(
                open_y, whole(ref, 1, x - shift) - (press_ref[x, 1 : block_y + 1, :] - here), 0.0
            )
            out_ref[x, 2] = jnp.where(
                open_z, whole(ref, 2, x - shift) - (pltpu.roll(here, size_z - 1, 1) - here), 0.0
            )
        for x in range(first, first + 4):
            out_copy(x).start()

    for first, ref, shift in (
        (0, lifted_ref, 0),
        (4, lifted_in_ref, 4),
        (8, lifted_in_ref, 4),
        (12, lifted_ref, 8),
    ):
        finish(ref, shift, first)

    def drain(x, carry):
        glow_copy(x).wait()
        out_copy(x).wait()
        return carry

    lax.fori_loop(0, block_x, drain, 0)


def shaped(*dims):
    return jax.ShapeDtypeStruct(dims, jnp.float32)


def call(kernel, outs, scratch, grant, spaces={}, outside=0):
    vmem = pl.BlockSpec(memory_space=pltpu.VMEM)

    def run(*args):
        specs = [
            pl.BlockSpec(memory_space=spaces[at]) if at in spaces else vmem
            for at in range(len(args))
        ]
        places = [
            pl.BlockSpec(memory_space=pltpu.HBM) if at < outside else vmem
            for at in range(len(jax.tree.leaves(outs)))
        ]
        return pl.pallas_call(
            kernel,
            out_shape=outs,
            in_specs=specs,
            out_specs=jax.tree.unflatten(jax.tree.structure(outs), places),
            scratch_shapes=[
                pltpu.VMEM(entry, jnp.float32) if isinstance(entry, tuple) else entry
                for entry in scratch
            ],
            compiler_params=pltpu.CompilerParams(vmem_limit_bytes=grant << 20),
            cost_estimate=pl.CostEstimate(
                flops=10**9, bytes_accessed=1024, transcendentals=0
            ),
        )(*args)

    return run


inputs_here = [
    pltpu.VMEM((3, block_x, block_y, size_z), jnp.bfloat16),
    pltpu.VMEM((block_x, block_y, size_z), jnp.bfloat16),
    pltpu.SemaphoreType.DMA((2,)),
]


def fetched(velocity_hbm, density_hbm, velocity_ref, density_ref, arrived):
    return [
        pltpu.make_async_copy(velocity_hbm, velocity_ref, arrived.at[0]),
        pltpu.make_async_copy(density_hbm, density_ref, arrived.at[1]),
    ]


def step(velocity, density, rims):
    table_z = cosine_array(size_z)
    table_x = cosine_array(full_x)
    eigen_z = jnp.asarray(eigen_array(size_z))
    eigen_x = jnp.asarray(np.broadcast_to(eigen_array(full_x)[None, :], (chunk_z, full_x)))
    low_x, high_x, low_y, high_y, low_c, high_c = rims
    here = {0: pltpu.HBM, 1: pltpu.HBM, 2: pltpu.HBM, 3: pltpu.HBM}
    thick, plane = (2, 9, 8, 128), (2, 48, 128)
    one, lifted_in, smoke_in, div_in, ends = call(
        inner_kernel,
        (
            shaped(4, 8, *thick),
            shaped(3, 8, *plane),
            shaped(8, *plane),
            shaped(8, *plane),
            shaped(2, 2, tiles, 8, 128),
        ),
        [
            (4, block_x, *plane),
            (4, block_x, *thick),
            (4, 12, *thick),
            (3, 8, *plane),
            (8, *plane),
            (8, *plane),
            (4, 2, tiles, 8, 128),
            pltpu.SemaphoreType.DMA((2,)),
            pltpu.SemaphoreType.DMA((3, 8)),
            *inputs_here,
        ],
        20,
        {0: pltpu.HBM, 1: pltpu.HBM},
        outside=4,
    )(velocity, density, low_y, high_y)
    lifted, smoke, packed = call(
        outer_kernel,
        (shaped(3, 8, *plane), shaped(8, *plane), shaped(count_x * send_rows, 128)),
        [
            (4, block_x + 9, *plane),
            (4, block_x + 9, *thick),
            (4, block_x + 5, *thick),
            (2, 2, tiles, 8, 128),
            (block_x, *plane),
            (block_x * block_y, size_z),
            plane,
            (4, 2, tiles, 8, 128),
            pltpu.SemaphoreType.DMA((3,)),
            *inputs_here,
        ],
        25,
        here,
    )(
        velocity, density, one, div_in, ends, low_x, high_x, low_y, high_y, low_c, high_c,
        table_side(table_z.T[:, turned], 0, 2),
    )
    got = lax.all_to_all(
        packed.reshape(count_x, send_rows, 128), "gx", split_axis=0, concat_axis=0, tiled=True
    )
    local, ends, moments, before = call(
        forward_kernel,
        (
            shaped(block_y * chunk_z, full_x),
            shaped(2, chunk_z, full_x),
            shaped(count_y, chunk_z, full_x),
            shaped(count_x, 8, 128),
        ),
        [(block_y * chunk_z, full_x)],
        4,
        {0: pltpu.SMEM},
    )(eigen_z, got, eigen_x, table_side(table_x.T, 0, 2))
    moments = lax.all_to_all(moments, "gy", split_axis=0, concat_axis=0, tiled=True)
    back = call(
        backward_kernel,
        shaped(count_x, back_rows, 128),
        [(5 * 128, full_x)],
        4,
        {0: pltpu.SMEM},
    )(eigen_z, local, ends, moments, eigen_x, table_side(table_x.T, 1, 3), before)
    back = lax.all_to_all(back, "gx", split_axis=0, concat_axis=0, tiled=True)
    return call(
        final_kernel,
        (shaped(3, block_x, block_y, size_z), shaped(block_x, block_y, size_z)),
        [
            (block_x + 1, 40, size_z),
            (block_x + 1, 40, size_z),
            (block_x, 3, block_y, size_z),
            (block_x, block_y, size_z),
            pltpu.SemaphoreType.DMA((block_x,)),
            pltpu.SemaphoreType.DMA((block_x,)),
        ],
        8,
        outside=2,
    )(
        back.reshape(count_x * back_rows, 128), lifted, lifted_in, smoke, smoke_in,
        table_side(table_z, 0, 3),
    )


def moved(part, axis, upward):
    pairs = [(i, i + 1) if upward else (i + 1, i) for i in range(15)]
    return lax.ppermute(part, axis, pairs)


def per_device(velocity, density):
    planes, rows = (2, block_y, 128), (block_x // 2, 2, 8, 128)
    up_x, down_x, up_y, down_y = call(
        edge_kernel,
        (shaped(17, *planes), shaped(16, *planes), shaped(5, *rows), shaped(4, *rows)),
        inputs_here,
        4,
        {0: pltpu.HBM, 1: pltpu.HBM},
    )(
        pltpu.with_memory_space_constraint(velocity, pltpu.HBM),
        pltpu.with_memory_space_constraint(density, pltpu.HBM),
    )
    low_x = moved(up_x, "gx", True)
    high_x = moved(down_x, "gx", False)
    low_y = moved(up_y, "gy", True)
    high_y = moved(down_y, "gy", False)
    corner = shaped(len(corner_tiles), 2, 8, 128)
    up_c, down_c = call(corner_kernel, (corner, corner), [], 2)(low_y, high_y)
    low_c = moved(up_c, "gx", True)
    high_c = moved(down_c, "gx", False)
    return step(velocity, density, (low_x, high_x, low_y, high_y, low_c, high_c))


def solution(mesh):
    in_specs = (P(None, "gx", "gy", None), P("gx", "gy", None))
    out_specs = (P(None, "gx", "gy", None), P("gx", "gy", None))
    return jax.shard_map(
        per_device, mesh=mesh, in_specs=in_specs, out_specs=out_specs, check_vma=False
    )
```

```python
import jax
import jax.numpy as jnp
import numpy as np
from jax import lax
from jax.experimental import pallas as pl
from jax.experimental.pallas import tpu as pltpu
from jax.sharding import PartitionSpec as P

time_step = 0.4
buoyancy = 2.0
extinction = 3.0

block_x, block_y, size_z = 16, 32, 256
count_x, count_y = 16, 16
full_x, full_y = 256, 512
chunk_z = 16
send_rows = 72
back_rows = 88


def cosine_array(length):
    modes = np.arange(length, dtype=np.float64)[:, None]
    centres = np.arange(length, dtype=np.float64)[None, :] + 0.5
    factor = np.where(modes == 0, np.sqrt(1.0 / length), np.sqrt(2.0 / length))
    return (factor * np.cos(np.pi * modes * centres / length)).astype(np.float32)


def eigen_array(length):
    modes = np.arange(length, dtype=np.float64)
    return (4.0 * np.sin(np.pi * modes / (2 * length)) ** 2).astype(np.float32)


def swap_groups(tile):
    row = lax.broadcasted_iota(jnp.int32, (8, 128), 0)
    group = lax.broadcasted_iota(jnp.int32, (8, 128), 1) // 16
    skewed = pltpu.roll(tile, 0, 1, stride=16, stride_axis=0)
    upturned = pltpu.roll(
        jnp.take_along_axis(skewed, (row + group + 1) & 7, axis=0), 16, 1, stride=16, stride_axis=0
    )
    return jnp.take_along_axis(upturned, 7 - row, axis=0)


def turn_groups(tile):
    row = lax.broadcasted_iota(jnp.int32, (8, 128), 0)
    group = lax.broadcasted_iota(jnp.int32, (8, 128), 1) // 16
    skewed = pltpu.roll(tile, 0, 1, stride=16, stride_axis=0)
    return pltpu.roll(
        jnp.take_along_axis(skewed, (row + group) & 7, axis=0), 0, 1, stride=16, stride_axis=0
    )


turned = [half * 128 + (-group % 8) * 16 + mode for half in range(2) for group in range(8) for mode in range(16)]


def parts_of(value, count):
    found = []
    for _ in range(count):
        found.append(value.astype(jnp.bfloat16))
        value = value - found[-1].astype(np.float32)
    return found


pairs_of = {2: ((0, 0), (0, 1), (1, 0)), 3: ((0, 0), (0, 1), (1, 0), (0, 2), (2, 0), (1, 1))}


def data_side(value, axis, count):
    found = parts_of(value, count)
    return jnp.concatenate([found[at] for at, _ in pairs_of[count]], axis=axis)


def table_side(table, axis, count):
    found = parts_of(table, count)
    return jnp.asarray(np.concatenate([found[at] for _, at in pairs_of[count]], axis=axis))


def dot(left, right, dims):
    return lax.dot_general(left, right, (dims, ((), ())), preferred_element_type=jnp.float32)


def weights(speeds, step, half, lane):
    taps = []
    centre = None
    for axis, speed in enumerate(speeds):
        scaled = speed * (step / 6.0)
        ahead = jnp.maximum(scaled, 0.0)
        back = ahead - scaled
        both = ahead + back
        centre = both if centre is None else centre + both
        plus_two, minus_two = back, ahead
        plus_one = 6.0 * back - 2.0 * ahead
        minus_one = 6.0 * ahead - 2.0 * back
        if axis == 2 and half == 0:
            minus_one = jnp.where(lane > 0, minus_one, 0.0)
            minus_two = jnp.where(lane > 1, minus_two, 0.0)
        if axis == 2 and half == 1:
            plus_one = jnp.where(lane < 127, plus_one, 0.0)
            plus_two = jnp.where(lane < 126, plus_two, 0.0)
        taps.append((plus_two, plus_one, minus_one, minus_two))
    return taps, -3.0 * centre


def moved_along_z(pair, half, shift, lane):
    here = pltpu.roll(pair[half], (128 - shift) % 128, 1)
    if (shift > 0) == (half == 1):
        return here
    other = pltpu.roll(pair[1 - half], (128 - shift) % 128, 1)
    return jnp.where(lane < 128 - shift if shift > 0 else lane >= -shift, here, other)


def change(ref, field, x, tile, half, pair, taps, centre, lane):
    total = centre * pair[half]
    for axis, (plus_two, plus_one, minus_one, minus_two) in enumerate(taps):
        if axis == 0:
            parts = [ref[field, x + shift, half, tile] for shift in (2, 1, -1, -2)]
        elif axis == 1:
            parts = [ref[field, x, half, tile + shift] for shift in (2, 1, -1, -2)]
        else:
            parts = [moved_along_z(pair, half, shift, lane) for shift in (2, 1, -1, -2)]
        total = total - plus_two * parts[0]
        total = total + plus_one * parts[1]
        total = total + minus_one * parts[2]
        total = total - minus_two * parts[3]
    return total


tiles = 5
halves = range(2)


def rows_of_tile(tile):
    return pl.ds(3 + tile, 8, stride=5)


def stencil(raw_ref, raw_first, one_ref, one_first):
    place_x, place_y = lax.axis_index("gx"), lax.axis_index("gy")
    lane = lax.broadcasted_iota(jnp.int32, (8, 128), 1)
    last_row = (lax.broadcasted_iota(jnp.int32, (8, 128), 0) == 7) & (place_y == count_y - 1)

    def closed(value, field, open_x, tile, half):
        if field == 0:
            return jnp.where(open_x, value, 0.0)
        if field == 1 and tile == 1:
            return jnp.where(last_row, 0.0, value)
        if field == 2 and half == 1:
            return jnp.where(lane < 127, value, 0.0)
        return value

    def is_open(x):
        return place_x * block_x + x != full_x - 1

    def section_one(x, fields=(0, 1, 2, 3)):
        at = x - raw_first
        for tile in range(tiles):
            pairs = [[raw_ref[field, at, half, tile + 2] for half in halves] for field in range(4)]
            for half in halves:
                taps, centre = weights([pairs[c][half] for c in range(3)], time_step, half, lane)
                for field in fields:
                    value = pairs[field][half] + change(
                        raw_ref, field, at, tile + 2, half, pairs[field], taps, centre, lane
                    )
                    value = closed(value, field, is_open(x), tile, half)
                    one_ref[field, x - one_first, half, tile + 2] = value
                    if tile < 2:
                        one_ref[field, x - one_first, half, tile + 7] = pltpu.roll(value, 7, 0)
                    if tile > 2:
                        one_ref[field, x - one_first, half, tile - 3] = pltpu.roll(value, 1, 0)

    def section_two(x, tile, fields):
        at = x - one_first
        pairs = [[one_ref[field, at, half, tile + 2] for half in halves] for field in range(4)]
        values = {field: [] for field in fields}
        for half in halves:
            taps, centre = weights([pairs[c][half] for c in range(3)], 0.5 * time_step, half, lane)
            for field in fields:
                value = 0.5 * (
                    raw_ref[field, x - raw_first, half, tile + 2] + pairs[field][half]
                ) + change(one_ref, field, at, tile + 2, half, pairs[field], taps, centre, lane)
                values[field].append(closed(value, field, is_open(x), tile, half))
        return values

    def plane(x, at, div_at, lifted_ref, smoke_ref, div_ref, ends_ref, hold_ref):
        for tile in range(tiles):
            values = section_two(x, tile, (0, 1, 2, 3))
            for field in range(4):
                for half in halves:
                    hold_ref[field, half, tile] = values[field][half]
        for tile in range(tiles):
            rows = rows_of_tile(tile)
            along_x, along_y, along_z, smoke = (
                [hold_ref[field, half, tile] for half in halves] for field in range(4)
            )
            along_z = [
                along_z[half]
                + (time_step * buoyancy * 0.5)
                * (smoke[half] + moved_along_z(smoke, half, 1, lane))
                for half in halves
            ]
            along_z[1] = jnp.where(lane < 127, along_z[1], 0.0)
            for half in halves:
                ends_ref[1, half, tile] = ends_ref[1, half, tile] + smoke[half]
                beneath = moved_along_z(along_z, half, -1, lane)
                if half == 0:
                    beneath = jnp.where(lane > 0, beneath, 0.0)
                below_y = hold_ref[1, half, (tile - 1) % tiles]
                if tile == 0:
                    below_y = pltpu.roll(below_y, 1, 0)
                div_ref[div_at, half, rows, :] = (
                    along_x[half]
                    - ends_ref[0, half, tile]
                    + (along_z[half] - beneath)
                    + (along_y[half] - below_y)
                )
                ends_ref[0, half, tile] = along_x[half]
                lifted_ref[0, at, half, rows, :] = along_x[half]
                lifted_ref[1, at, half, rows, :] = along_y[half]
                lifted_ref[2, at, half, rows, :] = along_z[half]
                smoke_ref[at, half, rows, :] = smoke[half]

    return section_one, section_two, plane


def fill_plane(stage_ref, at, velocity_ref, density_ref, x):
    for field in range(4):
        source = (velocity_ref[field, x] if field < 3 else density_ref[x]).astype(jnp.float32)
        for half in halves:
            stage_ref[field, at, half, 8:40, :] = source[:, half * 128 : half * 128 + 128]


def fill_rims(stage_ref, at, low_y_ref, high_y_ref, pair):
    for field in range(4):
        for half in halves:
            low, high = low_y_ref[field, pair, half], high_y_ref[field, pair, half]
            stage_ref[field, at, half, 4:8, :] = low[0:4]
            stage_ref[field, at + 1, half, 4:8, :] = low[4:8]
            stage_ref[field, at, half, 40:44, :] = high[0:4]
            stage_ref[field, at + 1, half, 40:44, :] = high[4:8]


def fill_fifth(stage_ref, at, low_y_ref, x):
    for half in halves:
        stage_ref[1, at, half, 3:4, :] = low_y_ref[4, x // 8, half, x % 8 : x % 8 + 1, :]


def spread(stage_ref, raw_ref, x):
    for field in range(4):
        for half in halves:
            for tile in range(-2, tiles + 2):
                raw_ref[field, x, half, tile + 2] = stage_ref[field, x, half, rows_of_tile(tile), :]


def each(first, last, work):
    def one(x, carry):
        work(x)
        return carry

    lax.fori_loop(first, last, one, 0)


def inner_kernel(
    velocity_hbm, density_hbm, low_y_ref, high_y_ref, one_hbm, lifted_hbm, smoke_hbm, div_hbm, ends_ref,
    stage_ref, raw_ref, one_ref, lifted_ref, smoke_ref, div_ref, hold_ref, one_sent, plane_sent,
    velocity_ref, density_ref, arrived,
):
    copies = fetched(velocity_hbm, density_hbm, velocity_ref, density_ref, arrived)
    for copy in copies:
        copy.start()
    each(0, 8, lambda pair: fill_rims(stage_ref, 2 * pair, low_y_ref, high_y_ref, pair))
    for x in range(block_x):
        fill_fifth(stage_ref, x, low_y_ref, x)
    for copy in copies:
        copy.wait()
    each(0, block_x, lambda x: fill_plane(stage_ref, x, velocity_ref, density_ref, x))
    each(0, block_x, lambda x: spread(stage_ref, raw_ref, x))
    section_one, _, plane = stencil(raw_ref, 0, one_ref, 2)

    def both(step):
        section_one(2 * step + 2)
        section_one(2 * step + 3)

    each(0, 6, both)
    one_copies = [
        pltpu.make_async_copy(
            one_ref.at[:, 8 * part : 8 * part + 4], one_hbm.at[:, 4 * part : 4 * part + 4], one_sent.at[part]
        )
        for part in range(2)
    ]
    for copy in one_copies:
        copy.start()
    ends_ref[...] = jnp.zeros((2, 2, tiles, 8, 128), jnp.float32)

    def plane_copies(at):
        return (
            pltpu.make_async_copy(lifted_ref.at[:, at], lifted_hbm.at[:, at], plane_sent.at[0, at]),
            pltpu.make_async_copy(smoke_ref.at[at], smoke_hbm.at[at], plane_sent.at[1, at]),
            pltpu.make_async_copy(div_ref.at[at], div_hbm.at[at], plane_sent.at[2, at]),
        )

    def work(at):
        plane(at + 4, at, at, lifted_ref, smoke_ref, div_ref, ends_ref, hold_ref)
        for copy in plane_copies(at):
            copy.start()

    each(0, 8, work)

    def drain(at):
        for copy in plane_copies(at):
            copy.wait()

    each(0, 8, drain)
    for copy in one_copies:
        copy.wait()


def outer_kernel(
    velocity_hbm, density_hbm, one_hbm, div_hbm, inner_ends_ref, low_x_ref, high_x_ref, low_y_ref,
    high_y_ref, low_c_ref, high_c_ref, table_ref, lifted_ref, smoke_ref, out_ref,
    stage_ref, raw_ref, one_ref, ends_ref, div_ref, freq_ref, total_ref, hold_ref, one_arrived,
    velocity_ref, density_ref, arrived,
):
    copies = fetched(velocity_hbm, density_hbm, velocity_ref, density_ref, arrived)
    inner_copies = [
        pltpu.make_async_copy(
            one_hbm.at[:, 4 * part : 4 * part + 4],
            one_ref.at[:, 5 + 8 * part : 9 + 8 * part],
            one_arrived.at[part],
        )
        for part in range(2)
    ] + [pltpu.make_async_copy(div_hbm, div_ref.at[4:12], one_arrived.at[2])]
    for copy in copies + inner_copies:
        copy.start()
    for field in range(4):
        for x in range(4):
            for half in halves:
                for at, edge_ref in ((1, low_x_ref), (21, high_x_ref)):
                    stage_ref[field, x + at, half, 8:40, :] = edge_ref[field * 4 + x, half]
    for at, (field, planes) in enumerate(corner_tiles):
        for half in halves:
            for corner_ref, low in ((low_c_ref, True), (high_c_ref, False)):
                corner = corner_ref[at, half]
                for place, far in enumerate(planes):
                    x = 5 - far if low else 20 + far
                    if len(planes) == 1:
                        stage_ref[field, x, half, 4:8, :] = corner[4:8]
                        stage_ref[field, x, half, 40:44, :] = corner[0:4]
                    else:
                        stage_ref[field, x, half, 6:8, :] = corner[4 * place + 2 : 4 * place + 4]
                        stage_ref[field, x, half, 40:42, :] = corner[4 * place : 4 * place + 2]
    for half in halves:
        stage_ref[0, 0, half, 8:40, :] = low_x_ref[16, half]
    for pair in (0, 1, 6, 7):
        fill_rims(stage_ref, 2 * pair + 5, low_y_ref, high_y_ref, pair)
    for x in (0, 1, 2, 3, 12, 13, 14, 15):
        fill_fifth(stage_ref, x + 5, low_y_ref, x)
    for copy in copies:
        copy.wait()

    def fill(at):
        x = jnp.where(at < 4, at, at + 8)
        fill_plane(stage_ref, x + 5, velocity_ref, density_ref, x)

    each(0, 8, fill)
    section_one, section_two, plane = stencil(raw_ref, -5, one_ref, -3)

    each(0, 17, lambda at: spread(stage_ref, raw_ref, jnp.where(at < 9, at, at + 8)))
    section_one(-3, (0,))

    def both(step):
        x = jnp.where(step < 2, 2 * step - 2, 2 * step + 10)
        section_one(x)
        section_one(x + 1)

    each(0, 4, both)
    for copy in inner_copies:
        copy.wait()
    for tile in range(tiles):
        for half, value in enumerate(section_two(-1, tile, (0,))[0]):
            ends_ref[0, half, tile] = value
    ends_ref[1] = inner_ends_ref[1]
    each(0, 4, lambda x: plane(x, x, x, lifted_ref, smoke_ref, div_ref, ends_ref, hold_ref))
    for tile in range(tiles):
        for half in halves:
            rows = rows_of_tile(tile)
            div_ref[4, half, rows, :] = div_ref[4, half, rows, :] - ends_ref[0, half, tile]
    ends_ref[0] = inner_ends_ref[0]
    each(12, 16, lambda x: plane(x, x - 8, x, lifted_ref, smoke_ref, div_ref, ends_ref, hold_ref))
    for tile in range(tiles):
        for half in halves:
            total_ref[half, rows_of_tile(tile), :] = ends_ref[1, half, tile]
    lines = [div_ref[:, half, 8:40, :].reshape(block_x * block_y, 128) for half in halves]
    freq_ref[...] = dot(data_side(jnp.concatenate(lines, axis=1), 1, 2), table_ref[...], ((1,), (0,)))

    def pack(step):
        for x in range(4):
            x = step * 4 + x
            for part in range(4):
                for half in halves:
                    tile = freq_ref[
                        pl.ds(pl.multiple_of(x * block_y, 8) + part * 8, 8),
                        half * 128 : half * 128 + 128,
                    ]
                    out_ref[
                        pl.ds(half * 8 * send_rows + part * 16 + x, 8, stride=send_rows), :
                    ] = turn_groups(tile)

    each(0, block_x // 4, pack)
    for part in range(4):
        for half in halves:
            tile = total_ref[half, 8 + part * 8 : 16 + part * 8, :]
            out_ref[pl.ds(half * 8 * send_rows + 64 + part, 8, stride=send_rows), :] = swap_groups(
                tile
            )
    for peer in range(count_x):
        out_ref[peer * send_rows + 68 : peer * send_rows + 72, :] = jnp.zeros((4, 128), jnp.float32)


def edge_kernel(
    velocity_hbm, density_hbm, up_x_ref, down_x_ref, up_y_ref, down_y_ref,
    velocity_ref, density_ref, arrived,
):
    copies = fetched(velocity_hbm, density_hbm, velocity_ref, density_ref, arrived)
    for copy in copies:
        copy.start()
    for copy in copies:
        copy.wait()
    row = lax.broadcasted_iota(jnp.int32, (8, 128), 0)
    low_rows = row < 4

    def rows_of(field, x):
        return (velocity_ref[field, x] if field < 3 else density_ref[x]).astype(jnp.float32)

    for field in range(4):
        for x in range(4):
            top, bottom = rows_of(field, block_x - 4 + x), rows_of(field, x)
            for half in range(2):
                lanes = slice(half * 128, half * 128 + 128)
                up_x_ref[field * 4 + x, half] = top[:, lanes]
                down_x_ref[field * 4 + x, half] = bottom[:, lanes]
        for pair in range(block_x // 2):
            first, second = rows_of(field, 2 * pair), rows_of(field, 2 * pair + 1)
            for half in range(2):
                lanes = slice(half * 128, half * 128 + 128)
                up_y_ref[field, pair, half] = jnp.where(
                    low_rows,
                    pltpu.roll(first[block_y - 8 :, lanes], 4, 0),
                    second[block_y - 8 :, lanes],
                )
                down_y_ref[field, pair, half] = jnp.where(
                    low_rows, first[:8, lanes], pltpu.roll(second[:8, lanes], 4, 0)
                )
    for group in range(2):
        for half in range(2):
            lanes = slice(half * 128, half * 128 + 128)
            tile = jnp.zeros((8, 128), jnp.float32)
            for x in range(8):
                rows = rows_of(1, group * 8 + x)[block_y - 8 :, lanes]
                tile = jnp.where(row == x, pltpu.roll(rows, (x + 5) % 8, 0), tile)
            up_y_ref[4, group, half] = tile
    fifth = rows_of(0, block_x - 5)
    for half in range(2):
        up_x_ref[16, half] = fifth[:, half * 128 : half * 128 + 128]


corner_tiles = (
    (0, (1,)), (0, (2, 3)), (1, (1,)), (1, (2,)), (1, (3, 4)), (2, (1, 2)), (3, (1, 2)),
)


def corner_kernel(low_y_ref, high_y_ref, up_ref, down_ref):
    row = lax.broadcasted_iota(jnp.int32, (8, 128), 0)

    def rows_at(field, x, half):
        low, high = low_y_ref[field, x // 2, half], high_y_ref[field, x // 2, half]
        if x % 2 == 0:
            low = pltpu.roll(low, 4, 0)
        else:
            high = pltpu.roll(high, 4, 0)
        return jnp.where(row < 4, high, low)

    for at, (field, planes) in enumerate(corner_tiles):
        for half in halves:
            for ref, upward in ((up_ref, True), (down_ref, False)):
                found = [
                    rows_at(field, block_x - far if upward else far - 1, half) for far in planes
                ]
                if len(found) == 1:
                    ref[at, half] = found[0]
                else:
                    near, far = found
                    ref[at, half] = jnp.where(
                        row < 4,
                        jnp.where(row < 2, near, pltpu.roll(near, 4, 0)),
                        jnp.where(row < 6, pltpu.roll(far, 4, 0), far),
                    )


def power_of(base, exponent, bits):
    result = jnp.ones_like(base)
    for bit in range(bits):
        result = jnp.where((exponent >> bit) & 1 == 1, result * base, result)
        base = base * base
    return result


def roots_of(lam):
    half = 0.5 * lam
    spread = jnp.sqrt(lam + half * half)
    rho = 1.0 / (1.0 + half + spread)
    return rho, spread


def eigen_sum(eigen_ref, eigen_x_ref, place_x):
    row = lax.broadcasted_iota(jnp.int32, (chunk_z, full_x), 0)
    along_z = jnp.zeros((chunk_z, full_x), jnp.float32)
    for at in range(chunk_z):
        along_z = jnp.where(row == at, eigen_ref[place_x * chunk_z + at], along_z)
    return along_z + eigen_x_ref[...]


def squared(value, times):
    for _ in range(times):
        value = value * value
    return value


def forward_kernel(
    eigen_ref, got_ref, eigen_x_ref, table_ref, local_ref, ends_ref, send_ref, before_ref, line_ref
):
    place_x, place_y = lax.axis_index("gx"), lax.axis_index("gy")
    lines = [got_ref[:, part * 16 : part * 16 + 16, :].reshape(full_x, 128) for part in range(4)]
    line_ref[...] = dot(data_side(jnp.concatenate(lines, axis=1), 0, 2), table_ref[...], ((0,), (0,)))
    lam = eigen_sum(eigen_ref, eigen_x_ref, place_x)
    rho, _ = roots_of(lam)
    special = lam == 0.0
    low = jnp.zeros((chunk_z, full_x), jnp.float32)
    for y in range(block_y):
        low = low * rho + line_ref[y * 16 : y * 16 + 16, :]
        local_ref[y * 16 : y * 16 + 16, :] = low
    high = jnp.zeros((chunk_z, full_x), jnp.float32)
    for y in reversed(range(block_y)):
        high = high * rho
        rows = slice(y * 16, y * 16 + 16)
        here = local_ref[rows, :]
        local_ref[rows, :] = jnp.where(special, here, here + high)
        high = high + line_ref[rows, :]
    ends_ref[0] = low
    ends_ref[1] = high
    rho_32 = squared(rho, 5)
    rho_64 = rho_32 * rho_32
    up = low + power_of(rho_64, place_y, 4) * rho_32 * high
    down = high + power_of(rho_64, count_y - 1 - place_y, 4) * rho_32 * low
    for peer in range(count_y):
        send_ref[peer] = jnp.where(peer > place_y, up, down)
    running = jnp.zeros((4, 128), jnp.float32)
    for peer in range(count_x):
        before_ref[peer, 0:4, :] = running
        running = running + got_ref[peer, 64:68, :]


def turned_rows(y):
    at = (y // 8) * 128 + (-y % 8) * 16
    return slice(at, at + 16)


def backward_kernel(
    eigen_ref, local_ref, ends_ref, got_ref, eigen_x_ref, table_ref, before_ref, out_ref, line_ref
):
    place_x, place_y = lax.axis_index("gx"), lax.axis_index("gy")
    lam = eigen_sum(eigen_ref, eigen_x_ref, place_x)
    rho, spread = roots_of(lam)
    special = lam == 0.0
    scale = jnp.where(special, 0.0, -0.5 / jnp.where(special, 1.0, spread))
    low, high = ends_ref[0], ends_ref[1]
    rho_32 = squared(rho, 5)
    rho_64 = rho_32 * rho_32
    rho_up = power_of(rho_64, place_y, 4)
    rho_down = power_of(rho_64, count_y - 1 - place_y, 4)
    from_low = jnp.zeros((chunk_z, full_x), jnp.float32)
    from_high = jnp.zeros((chunk_z, full_x), jnp.float32)
    for peer in range(count_y):
        from_low = jnp.where(peer < place_y, from_low * rho_32 + got_ref[peer], from_low)
        other = count_y - 1 - peer
        from_high = jnp.where(other > place_y, from_high * rho_32 + got_ref[other], from_high)
    rho_992 = rho_up * rho_down * rho_32
    wrap = 1.0 / jnp.where(special, 1.0, 1.0 - rho_992 * rho_32)
    enter_low = (from_low + rho_up * (rho_32 * from_high + high) + rho_992 * low) * wrap
    enter_high = (from_high + rho_down * (rho_32 * from_low + low) + rho_992 * high) * wrap
    mean = (0.5 * (from_low + from_high) + low) * (1.0 / full_y)
    flux_in = 0.5 * from_low - mean * (place_y * block_y).astype(jnp.float32)
    for y in reversed(range(block_y)):
        enter_high_next = enter_high
        rows = slice((y + 1) * 16, (y + 1) * 16 + 16)
        if y + 1 == block_y:
            line_ref[turned_rows(y + 1), :] = rho * low + enter_high_next
        else:
            line_ref[turned_rows(y + 1), :] = local_ref[rows, :] + jnp.where(
                special, 0.0, enter_high_next
            )
        enter_high = enter_high * rho
    line_ref[0:16, :] = local_ref[0:16, :] + jnp.where(special, 0.0, enter_high)
    level = jnp.zeros((chunk_z, full_x), jnp.float32)
    for y in range(block_y + 1):
        rows = turned_rows(y)
        enter_low = enter_low * rho
        here = line_ref[rows, :]
        line_ref[rows, :] = jnp.where(special, level, scale * (here + enter_low))
        level = level + (here + flux_in - mean * (y + 1.0))
    line_ref[(block_y + 1) * 16 :, :] = jnp.zeros((112, full_x), jnp.float32)
    found = dot(table_ref[...], data_side(line_ref[...], 1, 3), ((1,), (1,)))
    for part in range(5):
        lanes = slice(part * 128, part * 128 + 128)
        out_ref[:, part * 16 : part * 16 + 16, :] = found[:, lanes].reshape(count_x, block_x, 128)
        if part < 4:
            for peer in range(count_x - 1):
                at = (peer + 1) * block_x
                out_ref[peer, 80 + part : 81 + part, :] = found[at : at + 1, lanes]
            out_ref[count_x - 1, 80 + part : 81 + part, :] = jnp.zeros((1, 128), jnp.float32)
    out_ref[:, 84:88, :] = before_ref[:, 0:4, :]


def final_kernel(
    got_ref, lifted_ref, lifted_in_ref, smoke_ref, smoke_in_ref, table_ref, out_hbm, glow_hbm,
    freq_ref, press_ref, out_ref, glow_ref, out_sent, glow_sent,
):
    place_x, place_y = lax.axis_index("gx"), lax.axis_index("gy")

    def tile_at(row, half, change=turn_groups):
        return change(got_ref[pl.ds(half * 8 * back_rows + row, 8, stride=back_rows), :])

    entered = jnp.concatenate(
        [
            jnp.concatenate([tile_at(84 + part, half, swap_groups) for half in range(2)], axis=1)
            for part in range(4)
        ],
        axis=0,
    )
    attenuation = extinction / full_x

    def whole(ref, *at):
        return jnp.concatenate([ref[(*at, half, slice(8, 40))] for half in range(2)], axis=1)

    def out_copy(x):
        return pltpu.make_async_copy(out_ref.at[x], out_hbm.at[:, x], out_sent.at[x])

    def glow_copy(x):
        return pltpu.make_async_copy(glow_ref.at[x], glow_hbm.at[x], glow_sent.at[x])

    def whole(ref, *at):
        return jnp.concatenate([ref[(*at, half, slice(8, 40))] for half in range(2)], axis=1)

    def shine(ref, shift, x, running):
        smoke = whole(ref, x - shift)
        depth = attenuation * smoke
        series = 1.0 - depth * (1.0 / 5.0)
        for order in (4.0, 3.0, 2.0):
            series = 1.0 - depth * (1.0 / order) * series
        lost = jnp.where(jnp.abs(depth) < 0.0625, depth * series, 1.0 - jnp.exp(-depth))
        glow_ref[x] = jnp.exp(-attenuation * running) * lost * (1.0 / attenuation)
        glow_copy(x).start()
        return running + smoke

    parts = ((0, 4, 0, lifted_ref, smoke_ref), (4, 12, 4, lifted_in_ref, smoke_in_ref),
             (12, 16, 8, lifted_ref, smoke_ref))
    for first, last, shift, _, ref in parts:
        for x in range(first, last):
            entered = shine(ref, shift, x, entered)

    def unpack(step):
        for x in range(4):
            x = step * 4 + x
            for part in range(5):
                for half in range(2):
                    freq_ref[x, part * 8 : part * 8 + 8, half * 128 : half * 128 + 128] = tile_at(
                        part * 16 + x, half
                    )

    each(0, block_x // 4, unpack)
    for part in range(4):
        for half in range(2):
            freq_ref[block_x, part * 8 : part * 8 + 8, half * 128 : half * 128 + 128] = tile_at(
                80 + part, half
            )
    freq_ref[block_x, 32:40, :] = jnp.zeros((8, size_z), jnp.float32)
    press_ref[...] = dot(
        data_side(freq_ref[...].reshape((block_x + 1) * 40, size_z), 1, 3), table_ref[...], ((1,), (0,))
    ).reshape(block_x + 1, 40, size_z)
    along_y = lax.broadcasted_iota(jnp.int32, (block_y, size_z), 0) + place_y * block_y
    along_z = lax.broadcasted_iota(jnp.int32, (block_y, size_z), 1)
    open_y = along_y < full_y - 1
    open_z = along_z < size_z - 1

    def finish(ref, shift, first):
        for x in range(first, first + 4):
            here = press_ref[x, 0:block_y, :]
            open_x = place_x * block_x + x < full_x - 1
            out_ref[x, 0] = jnp.where(
                open_x, whole(ref, 0, x - shift) - (press_ref[x + 1, 0:block_y, :] - here), 0.0
            )
            out_ref[x, 1] = jnp.where(
                open_y, whole(ref, 1, x - shift) - (press_ref[x, 1 : block_y + 1, :] - here), 0.0
            )
            out_ref[x, 2] = jnp.where(
                open_z, whole(ref, 2, x - shift) - (pltpu.roll(here, size_z - 1, 1) - here), 0.0
            )
        for x in range(first, first + 4):
            out_copy(x).start()

    for first, ref, shift in (
        (0, lifted_ref, 0),
        (4, lifted_in_ref, 4),
        (8, lifted_in_ref, 4),
        (12, lifted_ref, 8),
    ):
        finish(ref, shift, first)

    def drain(x, carry):
        glow_copy(x).wait()
        out_copy(x).wait()
        return carry

    lax.fori_loop(0, block_x, drain, 0)


def shaped(*dims):
    return jax.ShapeDtypeStruct(dims, jnp.float32)


def call(kernel, outs, scratch, grant, spaces={}, outside=0):
    vmem = pl.BlockSpec(memory_space=pltpu.VMEM)

    def run(*args):
        specs = [
            pl.BlockSpec(memory_space=spaces[at]) if at in spaces else vmem
            for at in range(len(args))
        ]
        places = [
            pl.BlockSpec(memory_space=pltpu.HBM) if at < outside else vmem
            for at in range(len(jax.tree.leaves(outs)))
        ]
        return pl.pallas_call(
            kernel,
            out_shape=outs,
            in_specs=specs,
            out_specs=jax.tree.unflatten(jax.tree.structure(outs), places),
            scratch_shapes=[
                pltpu.VMEM(entry, jnp.float32) if isinstance(entry, tuple) else entry
                for entry in scratch
            ],
            compiler_params=pltpu.CompilerParams(vmem_limit_bytes=grant << 20),
            cost_estimate=pl.CostEstimate(
                flops=10**9, bytes_accessed=1024, transcendentals=0
            ),
        )(*args)

    return run


inputs_here = [
    pltpu.VMEM((3, block_x, block_y, size_z), jnp.bfloat16),
    pltpu.VMEM((block_x, block_y, size_z), jnp.bfloat16),
    pltpu.SemaphoreType.DMA((2,)),
]


def fetched(velocity_hbm, density_hbm, velocity_ref, density_ref, arrived):
    return [
        pltpu.make_async_copy(velocity_hbm, velocity_ref, arrived.at[0]),
        pltpu.make_async_copy(density_hbm, density_ref, arrived.at[1]),
    ]


def step(velocity, density, rims):
    table_z = cosine_array(size_z)
    table_x = cosine_array(full_x)
    eigen_z = jnp.asarray(eigen_array(size_z))
    eigen_x = jnp.asarray(np.broadcast_to(eigen_array(full_x)[None, :], (chunk_z, full_x)))
    low_x, high_x, low_y, high_y, low_c, high_c = rims
    here = {0: pltpu.HBM, 1: pltpu.HBM, 2: pltpu.HBM, 3: pltpu.HBM}
    thick, plane = (2, 9, 8, 128), (2, 48, 128)
    one, lifted_in, smoke_in, div_in, ends = call(
        inner_kernel,
        (
            shaped(4, 8, *thick),
            shaped(3, 8, *plane),
            shaped(8, *plane),
            shaped(8, *plane),
            shaped(2, 2, tiles, 8, 128),
        ),
        [
            (4, block_x, *plane),
            (4, block_x, *thick),
            (4, 12, *thick),
            (3, 8, *plane),
            (8, *plane),
            (8, *plane),
            (4, 2, tiles, 8, 128),
            pltpu.SemaphoreType.DMA((2,)),
            pltpu.SemaphoreType.DMA((3, 8)),
            *inputs_here,
        ],
        20,
        {0: pltpu.HBM, 1: pltpu.HBM},
        outside=4,
    )(velocity, density, low_y, high_y)
    lifted, smoke, packed = call(
        outer_kernel,
        (shaped(3, 8, *plane), shaped(8, *plane), shaped(count_x * send_rows, 128)),
        [
            (4, block_x + 9, *plane),
            (4, block_x + 9, *thick),
            (4, block_x + 5, *thick),
            (2, 2, tiles, 8, 128),
            (block_x, *plane),
            (block_x * block_y, size_z),
            plane,
            (4, 2, tiles, 8, 128),
            pltpu.SemaphoreType.DMA((3,)),
            *inputs_here,
        ],
        25,
        here,
    )(
        velocity, density, one, div_in, ends, low_x, high_x, low_y, high_y, low_c, high_c,
        table_side(table_z.T[:, turned], 0, 2),
    )
    got = lax.all_to_all(
        packed.reshape(count_x, send_rows, 128), "gx", split_axis=0, concat_axis=0, tiled=True
    )
    local, ends, moments, before = call(
        forward_kernel,
        (
            shaped(block_y * chunk_z, full_x),
            shaped(2, chunk_z, full_x),
            shaped(count_y, chunk_z, full_x),
            shaped(count_x, 8, 128),
        ),
        [(block_y * chunk_z, full_x)],
        4,
        {0: pltpu.SMEM},
    )(eigen_z, got, eigen_x, table_side(table_x.T, 0, 2))
    moments = lax.all_to_all(moments, "gy", split_axis=0, concat_axis=0, tiled=True)
    back = call(
        backward_kernel,
        shaped(count_x, back_rows, 128),
        [(5 * 128, full_x)],
        4,
        {0: pltpu.SMEM},
    )(eigen_z, local, ends, moments, eigen_x, table_side(table_x.T, 1, 3), before)
    back = lax.all_to_all(back, "gx", split_axis=0, concat_axis=0, tiled=True)
    return call(
        final_kernel,
        (shaped(3, block_x, block_y, size_z), shaped(block_x, block_y, size_z)),
        [
            (block_x + 1, 40, size_z),
            (block_x + 1, 40, size_z),
            (block_x, 3, block_y, size_z),
            (block_x, block_y, size_z),
            pltpu.SemaphoreType.DMA((block_x,)),
            pltpu.SemaphoreType.DMA((block_x,)),
        ],
        8,
        outside=2,
    )(
        back.reshape(count_x * back_rows, 128), lifted, lifted_in, smoke, smoke_in,
        table_side(table_z, 0, 3),
    )


def moved(part, axis, upward):
    pairs = [(i, i + 1) if upward else (i + 1, i) for i in range(15)]
    return lax.ppermute(part, axis, pairs)


def per_device(velocity, density):
    planes, rows = (2, block_y, 128), (block_x // 2, 2, 8, 128)
    up_x, down_x, up_y, down_y = call(
        edge_kernel,
        (shaped(17, *planes), shaped(16, *planes), shaped(5, *rows), shaped(4, *rows)),
        inputs_here,
        4,
        {0: pltpu.HBM, 1: pltpu.HBM},
    )(
        pltpu.with_memory_space_constraint(velocity, pltpu.HBM),
        pltpu.with_memory_space_constraint(density, pltpu.HBM),
    )
    low_x = moved(up_x, "gx", True)
    high_x = moved(down_x, "gx", False)
    low_y = moved(up_y, "gy", True)
    high_y = moved(down_y, "gy", False)
    corner = shaped(len(corner_tiles), 2, 8, 128)
    up_c, down_c = call(corner_kernel, (corner, corner), [], 2)(low_y, high_y)
    low_c = moved(up_c, "gx", True)
    high_c = moved(down_c, "gx", False)
    return step(velocity, density, (low_x, high_x, low_y, high_y, low_c, high_c))


def solution(mesh):
    in_specs = (P(None, "gx", "gy", None), P("gx", "gy", None))
    out_specs = (P(None, "gx", "gy", None), P("gx", "gy", None))
    return jax.shard_map(
        per_device, mesh=mesh, in_specs=in_specs, out_specs=out_specs, check_vma=False
    )
```
